256 devices in a mesh: ctx: 32 (over y_lo, z, core), mp: 8 (over y_hi, x).
Axes of the slice: x: 4, y: 4 (y_hi: 2, y_lo: 2; y = y_hi * 2 + y_lo), z: 8, core: 2. Of those that a mesh axis runs over, the one named last changes fastest.
Arguments:
- tokens: bfloat16 [24576, 4096], P('ctx', 'mp'), may hold values from -20 to 20
- norm_gain: float32 [4096], P('mp'), may hold values from 0.5 to 1.5
- in_weight: bfloat16 [4096, 3, 4096], P('ctx', None, 'mp'), may hold values from -0.09375 to 0.09375
- short_weight: float32 [3, 3, 4096], P(None, None, 'mp'), may hold values from -3.5 to 3.5
- filters: bfloat16 [128, 256], P(None, 'mp'), may hold values from -0.5 to 0.5
- skip: float32 [4096], P('mp'), may hold values from -4 to 4
- out_weight: bfloat16 [4096, 4096], P('ctx', 'mp'), may hold values from -0.09375 to 0.09375
Outputs:
- block_out: bfloat16 [24576, 4096], P('ctx', 'mp')
The draws below stay inside these ranges and needn't reach their ends.
All inputs are finite; a program needn't handle non-finite values.
Results may differ from the reference program's by a relative error of at most 0.022.
Values may be sent and summed in bfloat16 or wider, within the bound.
A program may use at most 64 MiB of HBM per device.

```python
import jax
import jax.numpy as jnp
from jax import lax

D = 4096
FILT = 128
SHORT = 3
TOKENS = 24576
GROUPS = 256


def draw_tokens(key, part):
    inner = jax.random.fold_in(key, 11)
    first_key = jax.random.fold_in(inner, 0)
    channel_scale = 3.0 ** (jnp.arange(D, dtype=jnp.float32) / D)
    base = jax.random.truncated_normal(first_key, -6.0, 6.0, (TOKENS, D), jnp.float32)
    return (base * channel_scale).astype(jnp.bfloat16)


def level_of(own_key, shape, shards, low, largest):
    def one(axis_at, shards_of):
        steps = jax.random.uniform(jax.random.fold_in(jax.random.fold_in(own_key, 6), axis_at), (shards_of,), jnp.float32, low / len(shards), largest / len(shards))
        return jnp.repeat(jnp.exp(steps), shape[axis_at] // shards_of).reshape((-1,) + (1,) * (len(shape) - axis_at - 1))

    gain = one(*shards[0])
    for cut in shards[1:]:
        gain = gain * one(*cut)
    return gain


def noise(rng, dims, deviation, limit, pieces=(), held_as=jnp.bfloat16):
    values = deviation * jax.random.normal(rng, dims, jnp.float32)
    if pieces:
        values = values * level_of(rng, dims, pieces, -0.22, 0.18)
    return jnp.clip(values, -limit, limit).astype(held_as)


def setup_inputs(seed: int = 0) -> dict:
    key_list = jax.random.split(jax.random.key(seed), 8)
    return {
        "tokens": draw_tokens(jax.random.fold_in(key_list[7], 71), 0),
        "norm_gain": jnp.clip(0.5 + 1.0 * jax.random.uniform(key_list[1], (D,), jnp.float32) ** level_of(key_list[1], (D,), ((0, 8),), -0.2, 0.2), 0.5, 1.5),
        "in_weight": noise(key_list[2], (D, 3, D), D ** -0.5, 0.09375, ((0, 32), (2, 8))),
        "short_weight": noise(key_list[3], (SHORT, 3, D), SHORT ** -0.5, 3.5, ((2, 8),), jnp.float32),
        "filters": noise(key_list[4], (FILT, GROUPS), FILT ** -0.5, 0.5, ((1, 8),)),
        "skip": noise(key_list[5], (D,), 1.0, 4.0, ((0, 8),), jnp.float32),
        "out_weight": noise(key_list[6], (D, D), D ** -0.5, 0.09375, ((0, 32), (1, 8))),
    }


epsilon = 1e-06

def short_filter(padded, weight):
    taps = weight.shape[0]
    span = padded.shape[0] - (taps - 1)
    total = jnp.zeros((span,) + padded.shape[1:], jnp.float32)
    for tap in range(taps):
        begin = taps - 1 - tap
        total = total + weight[tap] * padded[begin:begin + span].astype(jnp.float32)
    return total

def medium_filter(gated, filters, count):
    taps = filters.shape[0]
    groups = filters.shape[1]
    size = gated.shape[1] // groups
    grouped = gated.reshape(gated.shape[0], groups, size)
    extended = jnp.pad(grouped, ((0, 1), (0, 0), (0, 0)))
    blocks = count // taps
    first = extended[:count].reshape(blocks, taps, groups, size)
    second = extended[taps:count + taps].reshape(blocks, taps, groups, size)
    windows = jnp.concatenate([first, second], axis=1).astype(jnp.float32)
    row_idx = jnp.arange(taps, dtype=jnp.int32)[:, None]
    col_idx = jnp.arange(2 * taps, dtype=jnp.int32)[None, :]
    offset = row_idx + taps - 1 - col_idx
    onehot = (offset[:, :, None] == jnp.arange(taps, dtype=jnp.int32)[None, None, :]).astype(jnp.float32)
    toeplitz = jnp.einsum('rwi,ig->rwg', onehot, filters.astype(jnp.float32))
    result = jnp.einsum('rwg,bwgk->brgk', toeplitz, windows)
    return result.reshape(count, groups * size)

def hyena_mix(padded, short_weight, filters, skip, count):
    taps = filters.shape[0]
    shorted = short_filter(padded, short_weight)
    query = shorted[taps - 1:, 0]
    gated = (shorted[:, 1] * shorted[:, 2]).astype(jnp.bfloat16)
    medium = medium_filter(gated, filters, count)
    direct = gated[taps - 1:].astype(jnp.float32)
    return (query * (medium + skip * direct)).astype(jnp.bfloat16)

def reference(tokens, norm_gain, in_weight, short_weight, filters, skip, out_weight):
    token_f = tokens.astype(jnp.float32)
    squares = lax.optimization_barrier(jnp.sum(token_f * token_f, axis=1))
    scale = lax.rsqrt(squares / D + epsilon)
    normed = (token_f * scale[:, None] * norm_gain).astype(jnp.bfloat16)
    streams = jnp.dot(normed, in_weight.reshape(D, 3 * D), preferred_element_type=jnp.float32)
    streams = streams.astype(jnp.bfloat16).reshape(TOKENS, 3, D)
    reach = FILT + SHORT - 2
    padded = jnp.pad(streams, ((reach, 0), (0, 0), (0, 0)))
    mixed = hyena_mix(padded, short_weight, filters, skip, TOKENS)
    branch = jnp.dot(mixed, out_weight, preferred_element_type=jnp.float32)
    return (token_f + branch).astype(jnp.bfloat16)
```

```python
import jax
import jax.numpy as jnp
from jax import lax
from jax.sharding import PartitionSpec as P

D = 4096
FILT = 128
SHORT = 3


epsilon = 1e-06


def short_filter(padded, weight):
    taps = weight.shape[0]
    span = padded.shape[0] - (taps - 1)
    total = jnp.zeros((span,) + padded.shape[1:], jnp.float32)
    for tap in range(taps):
        begin = taps - 1 - tap
        total = total + weight[tap] * padded[begin : begin + span].astype(jnp.float32)
    return total


def medium_filter(gated, filters, count):
    taps = filters.shape[0]
    groups = filters.shape[1]
    size = gated.shape[1] // groups
    grouped = gated.reshape(gated.shape[0], groups, size)
    extended = jnp.pad(grouped, ((0, 1), (0, 0), (0, 0)))
    blocks = count // taps
    first = extended[:count].reshape(blocks, taps, groups, size)
    second = extended[taps : count + taps].reshape(blocks, taps, groups, size)
    windows = jnp.concatenate([first, second], axis=1)
    row_idx = jnp.arange(taps, dtype=jnp.int32)[:, None]
    col_idx = jnp.arange(2 * taps, dtype=jnp.int32)[None, :]
    offset = row_idx + taps - 1 - col_idx
    onehot = (offset[:, :, None] == jnp.arange(taps, dtype=jnp.int32)[None, None, :]).astype(
        jnp.bfloat16
    )
    toeplitz = jnp.einsum(
        "rwi,ig->rwg", onehot, filters, preferred_element_type=jnp.float32
    ).astype(jnp.bfloat16)
    result = jnp.einsum("rwg,bwgk->brgk", toeplitz, windows, preferred_element_type=jnp.float32)
    return result.reshape(count, groups * size)


def hyena_mix(padded, short_weight, filters, skip, count):
    taps = filters.shape[0]
    shorted = short_filter(padded, short_weight)
    query = shorted[taps - 1 :, 0]
    gated = (shorted[:, 1] * shorted[:, 2]).astype(jnp.bfloat16)
    medium = medium_filter(gated, filters, count)
    direct = gated[taps - 1 :].astype(jnp.float32)
    return (query * (medium + skip * direct)).astype(jnp.bfloat16)


def body(tokens, norm_gain, in_weight, short_weight, filters, skip, out_weight):
    tok_count, width = tokens.shape
    rows = lax.all_gather(tokens, "mp", axis=1, tiled=True)
    gain = lax.all_gather(norm_gain, "mp", axis=0, tiled=True)
    rows_f = rows.astype(jnp.float32)
    squares = jnp.sum(rows_f * rows_f, axis=1)
    scale = lax.rsqrt(squares / D + epsilon)
    normed = (rows_f * scale[:, None] * gain).astype(jnp.bfloat16)
    streams = jnp.einsum(
        "tk,qkc->tqc",
        normed,
        lax.all_gather(jnp.transpose(in_weight, (1, 0, 2)), "ctx", axis=1, tiled=True),
        preferred_element_type=jnp.float32,
    ).astype(jnp.bfloat16)
    reach = FILT + SHORT - 2
    ctx_count = lax.axis_size("ctx")
    halo = lax.ppermute(
        streams[tok_count - reach :], "ctx", [(i, i + 1) for i in range(ctx_count - 1)]
    )
    padded = jnp.concatenate([halo, streams], axis=0)
    mixed = hyena_mix(padded, short_weight, filters, skip, tok_count)
    mixed_rows = lax.all_gather(mixed, "mp", axis=1, tiled=True)
    branch = jnp.dot(
        mixed_rows,
        lax.all_gather(out_weight, "ctx", axis=0, tiled=True),
        preferred_element_type=jnp.float32,
    )
    return (tokens.astype(jnp.float32) + branch).astype(jnp.bfloat16)


def solution(mesh):
    return jax.shard_map(
        body,
        mesh=mesh,
        in_specs=(
            P("ctx", "mp"),
            P("mp"),
            P("ctx", None, "mp"),
            P(None, None, "mp"),
            P(None, "mp"),
            P("mp"),
            P("ctx", "mp"),
        ),
        out_specs=P("ctx", "mp"),
        check_vma=False,
    )
```

```python
import jax
import jax.numpy as jnp
from jax import lax
from jax.experimental import pallas as pl
from jax.experimental.pallas import tpu as pltpu
from jax.sharding import PartitionSpec as P

D = 4096
EPS = 1e-06
NX, NZ, NY = 4, 8, 2
ROWS, COLS, DEPTH = 768, 512, 128
BLK = 128
NB = ROWS // BLK
XROWS = ROWS + 16
HALF = 384
GSIZE = 16
BF = jnp.bfloat16
F32 = jnp.float32


def kernel(
    tok_ref, gain_ref, inw_ref, short_ref, filt_ref, skip_ref, outw_ref,
    out_ref,
    xg, ag, wg, wo, mx, acc, acc2, gated, toep, ext, ss, hs_send, hs_recv,
    xs, xr, ms, mr, wsend, wrecv, wsib, osend, orecv, osib, hs, hr,
):
    ctx = lax.axis_index("ctx")
    mp = lax.axis_index("mp")
    core = ctx % 2
    z = (ctx // 2) % NZ
    yl = ctx // (2 * NZ)
    x = mp % NX
    yh = mp // NX

    def at(yl_, z_, core_, yh_, x_):
        return ((yl_ * NZ + z_) * 2 + core_, yh_ * NX + x_)

    right = at(yl, z, core, yh, (x + 1) % NX)
    left = at(yl, z, core, yh, (x + NX - 1) % NX)
    across = at(yl, z, core, 1 - yh, x)
    up = at(yl, (z + 1) % NZ, core, yh, x)
    down = at(yl, (z + NZ - 1) % NZ, core, yh, x)
    beside = at(1 - yl, z, core, yh, x)
    sib = at(yl, z, 1 - core, yh, x)
    after = ((ctx + 1) % (4 * NZ), mp)
    before = ((ctx + 4 * NZ - 1) % (4 * NZ), mp)

    barrier = pltpu.get_barrier_semaphore()
    everyone = (right, left, across, up, down, beside, sib, after, before)
    for dev in everyone:
        pl.semaphore_signal(barrier, inc=1, device_id=dev, device_id_type=pl.DeviceIdType.MESH)

    own = mp
    xg[own, 0:ROWS, :] = tok_ref[...]
    gain = gain_ref[...]
    g_hi = gain.astype(BF).astype(F32)
    g_mid = (gain - g_hi).astype(BF).astype(F32)
    g_lo = gain - g_hi - g_mid
    which = lax.broadcasted_iota(jnp.int32, (16, COLS), 0)
    parts = jnp.where(which == 0, g_hi, jnp.where(which == 1, g_mid, jnp.where(which == 2, g_lo, 0.0)))
    xg[own, ROWS:XROWS, :] = parts.astype(BF)

    pl.semaphore_wait(barrier, len(everyone))

    sends = []

    def push(src, dst, ssem, rsem, dev):
        copy = pltpu.make_async_remote_copy(
            src_ref=src, dst_ref=dst, send_sem=ssem, recv_sem=rsem,
            device_id=dev, device_id_type=pl.DeviceIdType.MESH,
        )
        copy.start()
        sends.append(copy)

    def arrived(dst, ssem, rsem):
        pltpu.make_async_remote_copy(
            src_ref=dst, dst_ref=dst, send_sem=ssem, recv_sem=rsem,
            device_id=sib, device_id_type=pl.DeviceIdType.MESH,
        ).wait_recv()

    class Ring:
        def __init__(self, buf, ssem, rsem, halves):
            self.buf, self.ssem, self.rsem = buf, ssem, rsem
            self.halves = halves
            self.count = 0

        def view(self, plane, dx, half):
            slot = ((yh + plane) % NY) * NX + (x + dx) % NX
            begin, size = self.halves[half]
            return self.buf.at[slot, pl.ds(begin, size), :]

        def send(self, plane, dx, half, way):
            dev, shift = {"r": (right, 1), "l": (left, NX - 1), "y": (across, 0)}[way]
            there = (1, 0) if way == "y" else (plane, (dx + NX - shift) % NX)
            view = self.view(plane, dx, half)
            push(
                view, view, self.ssem.at[self.count],
                self.rsem.at[there[0], there[1], half], dev,
            )
            self.count += 1

        def wait(self, plane, dx, half):
            arrived(self.view(plane, dx, half), self.ssem.at[0], self.rsem.at[plane, dx, half])

    class Column:
        def __init__(self, src, view_of, ssem, rsem, sibsem):
            self.src, self.view_of = src, view_of
            self.ssem, self.rsem, self.sibsem = ssem, rsem, sibsem
            self.count = 0

        def view(self, plane, dz, parity, part=None):
            q = ((yl + plane) % NY) * NZ + (z + dz) % NZ
            return self.view_of(2 * q + parity, part)

        def send(self, plane, dz, way, part=None):
            dev, shift = {"u": (up, 1), "d": (down, NZ - 1), "y": (beside, 0), "s": (sib, 0)}[way]
            dst = self.view(plane, dz, core, part)
            src = self.src if plane == 0 and dz == 0 else dst
            if way == "s":
                rsem = self.sibsem.at[plane, dz]
            elif way == "y":
                rsem = self.rsem.at[1, 0]
            else:
                rsem = self.rsem.at[plane, (dz + NZ - shift) % NZ + (NZ // 2 if part == 1 else 0)]
            push(src, dst, self.ssem.at[self.count], rsem, dev)
            self.count += 1

        def wait(self, plane, dz, part=None):
            arrived(
                self.view(plane, dz, core, part), self.ssem.at[0],
                self.rsem.at[plane, dz + (NZ // 2 if part == 1 else 0)],
            )

        def wait_sib(self, plane, dz):
            arrived(self.view(plane, dz, 1 - core), self.ssem.at[0], self.sibsem.at[plane, dz])

        def start(self):
            for way in ("y", "u", "d", "s"):
                self.send(0, 0, way)

        def beside_in(self):
            self.wait(1, 0)
            for way in ("u", "d", "s"):
                self.send(1, 0, way)

        def hop(self, plane, dist):
            for dz, way, part in ((NZ - dist, "u", 0), (dist, "d", 1)):
                self.wait(plane, dz)
                self.send(plane, dz, way, part if dist == NZ // 2 - 1 else None)
                self.send(plane, dz, "s")

        def last(self, plane):
            self.wait(plane, NZ // 2, 0)
            self.wait(plane, NZ // 2, 1)
            self.send(plane, NZ // 2, "s")

    def w_view(c, part):
        begin, size = (c % 4) * DEPTH, DEPTH
        if part is not None:
            begin, size = begin + part * (DEPTH // 2), DEPTH // 2
        return wg.at[c // 4, :, pl.ds(begin, size), :]

    def o_view(c, part):
        begin, size = (c % 4) * DEPTH, DEPTH
        if part is not None:
            begin, size = begin + part * (DEPTH // 2), DEPTH // 2
        return wo.at[c // 4, pl.ds(begin, size), :]

    tok = Ring(xg, xs, xr, ((0, HALF), (HALF, XROWS - HALF)))
    mix = Ring(mx, ms, mr, ((HALF, HALF), (0, HALF)))
    win = Column(inw_ref, w_view, wsend, wrecv, wsib)
    wout = Column(outw_ref, o_view, osend, orecv, osib)

    win.start()
    for half, way in ((0, "y"), (0, "r"), (1, "l"), (1, "y"), (1, "r"), (0, "l")):
        tok.send(0, 0, half, way)

    wg[ctx // 4, :, pl.ds(pl.multiple_of((ctx % 4) * DEPTH, DEPTH), DEPTH), :] = inw_ref[...]
    wo[ctx // 4, pl.ds(pl.multiple_of((ctx % 4) * DEPTH, DEPTH), DEPTH), :] = outw_ref[...]
    acc[...] = jnp.zeros_like(acc)
    ss[...] = jnp.zeros_like(ss)
    acc2[...] = tok_ref[...].astype(F32)
    ext[:, 0:BLK] = filt_ref[...].astype(F32)
    ext[:, BLK:] = jnp.zeros((ext.shape[0], BLK), F32)

    @pl.loop(0, ext.shape[0])
    def _(g):
        row = jnp.broadcast_to(ext[pl.ds(g, 1), :], (2 * BLK, 2 * BLK))
        shifted = pltpu.roll(row, BLK, 1, stride=1, stride_axis=0)
        toep[pl.ds(pl.multiple_of(g * BLK, BLK), BLK), :] = shifted[:, 0:BLK].T.astype(BF)

    def norm(plane, dx):
        slot = ((yh + plane) % NY) * NX + (x + dx) % NX
        rows3 = xg[slot, ROWS:XROWS, :].astype(F32)
        g = rows3[0:1] + rows3[1:2] + rows3[2:3]

        @pl.loop(0, NB)
        def _(b):
            rows = pl.ds(pl.multiple_of(b * BLK, BLK), BLK)
            t = xg[slot, rows, :].astype(F32)
            sq = t * t
            ss[rows, :] += (sq[:, 0:128] + sq[:, 128:256]) + (sq[:, 256:384] + sq[:, 384:512])
            ag[slot, rows, :] = (t * g).astype(BF)

    norm(0, 0)

    win.beside_in()
    win.hop(0, 1)
    tok.wait(0, NX - 1, 0)
    tok.send(0, NX - 1, 0, "r")
    tok.wait(0, 1, 1)
    tok.send(0, 1, 1, "l")
    tok.wait(1, 0, 0)
    tok.send(1, 0, 0, "r")
    tok.wait(1, 0, 1)
    tok.send(1, 0, 1, "l")
    tok.send(1, 0, 1, "r")
    tok.send(1, 0, 0, "l")
    win.hop(1, 1)
    norm(1, 0)
    tok.wait(0, NX - 1, 1)
    norm(0, NX - 1)
    tok.wait(0, 1, 0)
    norm(0, 1)
    win.hop(0, 2)
    tok.wait(0, 2, 0)
    tok.wait(0, 2, 1)
    norm(0, 2)
    win.hop(1, 2)
    tok.wait(1, NX - 1, 0)
    tok.send(1, NX - 1, 0, "r")
    tok.wait(1, 1, 1)
    tok.send(1, 1, 1, "l")
    win.hop(0, 3)
    tok.wait(1, NX - 1, 1)
    norm(1, NX - 1)
    tok.wait(1, 1, 0)
    norm(1, 1)
    win.hop(1, 3)
    wout.start()
    tok.wait(1, 2, 0)
    tok.wait(1, 2, 1)
    norm(1, 2)
    for plane in range(NY):
        for dz in range(NZ):
            if dz != NZ // 2:
                win.wait_sib(plane, dz)

    def project(begin, count):
        @pl.loop(0, count * 3)
        def _(i):
            k = begin + i // 3
            s = i % 3
            plane, off = k % 2, k // 2
            off = jnp.where(off == 2, 3, jnp.where(off == 3, 2, off))
            m = ((yl + plane) % NY) * 4 + (z // 2 + off) % 4
            acc[s, 8 : 8 + ROWS, :] += jnp.dot(ag[m], wg[m, s], preferred_element_type=F32)

    project(0, 6)
    win.last(0)
    win.last(1)
    win.wait_sib(0, NZ // 2)
    win.wait_sib(1, NZ // 2)
    project(6, 2)

    wout.beside_in()
    wout.hop(0, 1)

    lanes_group = lax.broadcasted_iota(jnp.int32, (BLK, 128), 1) // GSIZE

    def taps(s, b, j):
        cols = slice(128 * j, 128 * (j + 1))
        v = acc[s, pl.ds(pl.multiple_of(b * BLK, BLK), BLK + 8), cols]
        total = short_ref[0, s : s + 1, cols] * v
        total = total + short_ref[1, s : s + 1, cols] * pltpu.roll(v, 1, 0)
        total = total + short_ref[2, s : s + 1, cols] * pltpu.roll(v, 2, 0)
        return total[8:]

    def settle(b):
        rows = pl.ds(pl.multiple_of(b * BLK, BLK), BLK)
        scale = lax.rsqrt(jnp.sum(ss[rows, :], axis=1, keepdims=True) / D + EPS)
        at_ = pl.ds(pl.multiple_of(b * BLK + 8, 8), BLK)
        for s in range(3):
            acc[s, at_, :] = (acc[s, at_, :] * scale).astype(BF).astype(F32)

    def gate(b):
        for j in range(4):
            kv = taps(1, b, j) * taps(2, b, j)
            gated[pl.ds(pl.multiple_of((b + 1) * BLK, BLK), BLK), 128 * j : 128 * (j + 1)] = kv.astype(BF)

    def combine(b):
        rows = pl.ds(pl.multiple_of(b * BLK, BLK), BLK)
        for j in range(4):
            cols = slice(128 * j, 128 * (j + 1))
            window = gated[pl.ds(pl.multiple_of(b * BLK, BLK), 2 * BLK), cols]
            every = jnp.dot(toep[1024 * j : 1024 * (j + 1), :], window, preferred_element_type=F32)
            medium = every[0:BLK]
            for g in range(1, 8):
                medium = jnp.where(lanes_group == g, every[BLK * g : BLK * (g + 1)], medium)
            direct = window[BLK:].astype(F32)
            mixed = taps(0, b, j) * (medium + skip_ref[:, cols] * direct)
            mx[own, rows, cols] = mixed.astype(BF)

    halo_g = (gated.at[pl.ds(ROWS, BLK), :], gated.at[pl.ds(0, BLK), :])

    def halo_out():
        for s in range(3):
            hs_send[s] = acc[s, ROWS - 8 : ROWS + 8, :].astype(BF)
        push(hs_send, hs_recv, hs.at[0], hr.at[0], after)
        push(halo_g[0], halo_g[1], hs.at[1], hr.at[1], after)

    def halo_in():
        arrived(hs_recv, hs.at[0], hr.at[0])
        arrived(halo_g[1], hs.at[1], hr.at[1])
        inside = ctx > 0
        for s in range(3):
            acc[s, 0:8, :] = jnp.where(inside, hs_recv[s].astype(F32)[8:16], 0.0)
        gated[0:BLK, :] = jnp.where(inside, gated[0:BLK, :].astype(F32), 0.0).astype(BF)

    settle(5)
    settle(4)
    gate(5)
    halo_out()
    settle(3)
    gate(4)
    combine(5)
    settle(2)
    gate(3)
    combine(4)
    settle(1)
    gate(2)
    combine(3)
    for way in ("y", "r", "l"):
        mix.send(0, 0, 0, way)
    settle(0)
    gate(1)
    combine(2)
    halo_in()
    gate(0)
    combine(1)
    combine(0)
    for way in ("y", "r", "l"):
        mix.send(0, 0, 1, way)

    def outward(plane, dx):
        slot = ((yh + plane) % NY) * NX + (x + dx) % NX
        acc2[...] += jnp.dot(mx[slot], wo[slot], preferred_element_type=F32)

    wout.hop(1, 1)
    mix.wait(0, NX - 1, 0)
    mix.send(0, NX - 1, 0, "r")
    mix.wait(1, 0, 0)
    mix.send(1, 0, 0, "r")
    mix.send(1, 0, 0, "l")
    wout.hop(0, 2)
    wout.hop(1, 2)
    mix.wait(0, 1, 1)
    mix.send(0, 1, 1, "l")
    mix.wait(1, 0, 1)
    mix.send(1, 0, 1, "r")
    mix.send(1, 0, 1, "l")
    wout.hop(0, 3)
    wout.hop(1, 3)
    wout.last(0)
    wout.last(1)
    for plane in range(NY):
        for dz in range(NZ):
            wout.wait_sib(plane, dz)
    mix.wait(0, NX - 1, 1)
    mix.wait(0, 1, 0)
    mix.wait(1, NX - 1, 0)
    mix.send(1, NX - 1, 0, "r")
    mix.wait(1, 1, 1)
    mix.send(1, 1, 1, "l")
    outward(0, 0)
    outward(1, 0)
    outward(0, NX - 1)
    outward(0, 1)
    mix.wait(0, 2, 0)
    mix.wait(0, 2, 1)
    outward(0, 2)
    mix.wait(1, NX - 1, 1)
    outward(1, NX - 1)
    mix.wait(1, 1, 0)
    outward(1, 1)
    mix.wait(1, 2, 0)
    mix.wait(1, 2, 1)
    outward(1, 2)
    out_ref[...] = acc2[...].astype(BF)
    for copy in sends:
        copy.wait_send()


def body(tokens, norm_gain, in_weight, short_weight, filters, skip, out_weight):
    vmem = pl.BlockSpec(memory_space=pltpu.VMEM)
    dma = pltpu.SemaphoreType.DMA
    return pl.pallas_call(
        kernel,
        out_shape=jax.ShapeDtypeStruct((ROWS, COLS), BF),
        in_specs=[vmem] * 7,
        out_specs=vmem,
        scratch_shapes=[
            pltpu.VMEM((8, XROWS, COLS), BF),
            pltpu.VMEM((8, ROWS, COLS), BF),
            pltpu.VMEM((8, 3, COLS, COLS), BF),
            pltpu.VMEM((8, COLS, COLS), BF),
            pltpu.VMEM((8, ROWS, COLS), BF),
            pltpu.VMEM((3, ROWS + 8, COLS), F32),
            pltpu.VMEM((ROWS, COLS), F32),
            pltpu.VMEM((ROWS + BLK, COLS), BF),
            pltpu.VMEM((32 * BLK, 2 * BLK), BF),
            pltpu.VMEM((32, 2 * BLK), F32),
            pltpu.VMEM((ROWS, 128), F32),
            pltpu.VMEM((3, 16, COLS), BF),
            pltpu.VMEM((3, 16, COLS), BF),
            dma((14,)), dma((2, 4, 2)),
            dma((14,)), dma((2, 4, 2)),
            dma((40,)), dma((2, 9)), dma((2, 8)),
            dma((40,)), dma((2, 9)), dma((2, 8)),
            dma((2,)), dma((2,)),
        ],
        compiler_params=pltpu.CompilerParams(
            collective_id=0, has_side_effects=True, vmem_limit_bytes=60 * 1024 * 1024
        ),
    )(
        tokens,
        norm_gain.reshape(1, COLS),
        jnp.transpose(in_weight, (1, 0, 2)),
        short_weight,
        filters.T,
        skip.reshape(1, COLS),
        out_weight,
    )


def solution(mesh):
    return jax.shard_map(
        body,
        mesh=mesh,
        in_specs=(
            P("ctx", "mp"),
            P("mp"),
            P("ctx", None, "mp"),
            P(None, None, "mp"),
            P(None, "mp"),
            P("mp"),
            P("ctx", "mp"),
        ),
        out_specs=P("ctx", "mp"),
        check_vma=False,
    )
```

```python
import jax
import jax.numpy as jnp
from jax import lax
from jax.experimental import pallas as pl
from jax.experimental.pallas import tpu as pltpu
from jax.sharding import PartitionSpec as P

D = 4096
EPS = 1e-06
NX, NZ, NY = 4, 8, 2
ROWS, COLS, DEPTH = 768, 512, 128
BLK = 128
NB = ROWS // BLK
XROWS = ROWS + 16
HALF = 384
GSIZE = 16
NEAR = 2
CHUNK = 2 * BLK
BF = jnp.bfloat16
F32 = jnp.float32


def kernel(
    tok_ref, gain_ref, inw_ref, short_ref, filt_ref, skip_ref, outw_ref,
    out_ref,
    xg, ag, wg, wo, yo, mx, acc, acc2, gated, toep, ext, ss, hs_send, hs_recv,
    part_send, part_recv, out_v, gain_v, short_v, filt_v, skip_v,
    ls, xs, xr, ms, mr, wsend, wrecv, wsib, osend, orecv, osib, ys, yr, ps, pr, hs, hr,
):
    ctx = lax.axis_index("ctx")
    mp = lax.axis_index("mp")
    core = ctx % 2
    z = (ctx // 2) % NZ
    yl = ctx // (2 * NZ)
    x = mp % NX
    yh = mp // NX

    def at(yl_, z_, core_, yh_, x_):
        return ((yl_ * NZ + z_) * 2 + core_, yh_ * NX + x_)

    right = at(yl, z, core, yh, (x + 1) % NX)
    left = at(yl, z, core, yh, (x + NX - 1) % NX)
    across = at(yl, z, core, 1 - yh, x)
    up = at(yl, (z + 1) % NZ, core, yh, x)
    down = at(yl, (z + NZ - 1) % NZ, core, yh, x)
    beside = at(1 - yl, z, core, yh, x)
    corner = at(1 - yl, z, core, 1 - yh, x)
    sib = at(yl, z, 1 - core, yh, x)
    after = ((ctx + 1) % (4 * NZ), mp)
    before = ((ctx + 4 * NZ - 1) % (4 * NZ), mp)

    barrier = pltpu.get_barrier_semaphore()
    everyone = (right, left, across, up, down, beside, corner, sib, after, before)
    for dev in everyone:
        pl.semaphore_signal(barrier, inc=1, device_id=dev, device_id_type=pl.DeviceIdType.MESH)

    own = mp
    row = yl * NZ + z
    my_rows = pl.ds(pl.multiple_of(core * DEPTH, DEPTH), DEPTH)
    loads = [
        pltpu.make_async_copy(src, dst, ls.at[i])
        for i, (src, dst) in enumerate((
            (inw_ref, wg.at[row, :, my_rows, :]),
            (tok_ref, xg.at[own, pl.ds(0, ROWS), :]),
            (gain_ref, gain_v),
            (outw_ref, yo.at[2 * yh + yl]),
            (filt_ref, filt_v),
            (short_ref, short_v),
            (skip_ref, skip_v),
        ))
    ]
    for copy in loads:
        copy.start()

    loads[2].wait()
    gain = gain_v[...]
    g_hi = gain.astype(BF).astype(F32)
    g_mid = (gain - g_hi).astype(BF).astype(F32)
    g_lo = gain - g_hi - g_mid
    which = lax.broadcasted_iota(jnp.int32, (16, COLS), 0)
    parts = jnp.where(which == 0, g_hi, jnp.where(which == 1, g_mid, jnp.where(which == 2, g_lo, 0.0)))
    xg[own, ROWS:XROWS, :] = parts.astype(BF)
    loads[0].wait()
    loads[1].wait()

    pl.semaphore_wait(barrier, len(everyone))

    sends = []

    def push(src, dst, ssem, rsem, dev):
        copy = pltpu.make_async_remote_copy(
            src_ref=src, dst_ref=dst, send_sem=ssem, recv_sem=rsem,
            device_id=dev, device_id_type=pl.DeviceIdType.MESH,
        )
        copy.start()
        sends.append(copy)

    def arrived(dst, ssem, rsem):
        pltpu.make_async_remote_copy(
            src_ref=dst, dst_ref=dst, send_sem=ssem, recv_sem=rsem,
            device_id=sib, device_id_type=pl.DeviceIdType.MESH,
        ).wait_recv()

    class Ring:
        def __init__(self, buf, planes, ssem, rsem, pieces):
            self.buf, self.planes = buf, planes
            self.ssem, self.rsem, self.pieces = ssem, rsem, pieces
            self.count = 0

        def slot(self, plane, dx):
            return ((yh + plane) % NY if self.planes == 2 else 0) * NX + (x + dx) % NX

        def view(self, plane, dx, piece):
            begin, size = self.pieces[piece]
            return self.buf.at[self.slot(plane, dx), pl.ds(begin, size), :]

        def send(self, plane, dx, piece, way):
            dev, shift = {"r": (right, 1), "l": (left, NX - 1), "y": (across, 0)}[way]
            there = (1, 0) if way == "y" else (plane, (dx + NX - shift) % NX)
            view = self.view(plane, dx, piece)
            push(
                view, view, self.ssem.at[self.count],
                self.rsem.at[there[0], there[1], piece], dev,
            )
            self.count += 1

        def wait(self, plane, dx, piece):
            arrived(self.view(plane, dx, piece), self.ssem.at[0], self.rsem.at[plane, dx, piece])

    class Column:
        def __init__(self, view_of, ssem, rsem, sibsem, near):
            self.view_of = view_of
            self.ssem, self.rsem, self.sibsem, self.near = ssem, rsem, sibsem, near
            self.count = 0

        def view(self, plane, dz, parity, part=None):
            begin, size = parity * DEPTH, DEPTH
            if part is not None:
                begin, size = begin + part * (DEPTH // 2), DEPTH // 2
            return self.view_of(plane, (z + dz) % NZ, pl.ds(begin, size))

        def send(self, plane, dz, way, part=None):
            dev, shift = {"u": (up, 1), "d": (down, NZ - 1), "y": (beside, 0), "s": (sib, 0)}[way]
            view = self.view(plane, dz, core, part)
            if way == "s":
                rsem = self.sibsem.at[plane, dz]
            elif way == "y":
                rsem = self.rsem.at[1, dz, 0]
            else:
                rsem = self.rsem.at[plane, (dz + NZ - shift) % NZ, part]
            push(view, view, self.ssem.at[self.count], rsem, dev)
            self.count += 1

        def wait(self, plane, dz, part=None):
            arrived(
                self.view(plane, dz, core, part), self.ssem.at[0],
                self.rsem.at[plane, dz, 0 if part is None else part],
            )

        def wait_sib(self, plane, dz):
            arrived(self.view(plane, dz, 1 - core), self.ssem.at[0], self.sibsem.at[plane, dz])

        def start(self, plane):
            for part in (0, 1):
                self.send(plane, 0, "u", part)
                self.send(plane, 0, "d", 1 - part)

        def hop(self, plane, dist):
            near = NZ // 2 if plane == 0 else self.near
            for turn in (0, 1):
                for dz, way, part in ((NZ - dist, "u", turn), (dist, "d", 1 - turn)):
                    self.wait(plane, dz, part)
                    if dist < near and (dist < NZ // 2 - 1 or turn == 0):
                        self.send(plane, dz, way, part)
            for dz in (NZ - dist, dist):
                self.out(plane, dz, dist)

        def out(self, plane, dz, dist):
            if plane == 0 and dist > self.near:
                self.send(0, dz, "y")
            self.send(plane, dz, "s")

        def last(self, plane):
            self.wait(plane, NZ // 2, 0)
            self.wait(plane, NZ // 2, 1)
            self.out(plane, NZ // 2, NZ // 2)

    tok = Ring(xg, 2, xs, xr, ((0, HALF), (HALF, XROWS - HALF)))
    mix = Ring(mx, 1, ms, mr, tuple((BLK * b, BLK) for b in range(NB)))
    win = Column(
        lambda plane, z_, rows: wg.at[((yl + plane) % NY) * NZ + z_, :, rows, :],
        wsend, wrecv, wsib, NEAR,
    )
    wout = Column(
        lambda plane, z_, rows: wo.at[plane, z_, rows, :],
        osend, orecv, osib, NZ // 2,
    )

    win.send(0, 0, "y")
    win.start(0)
    for half, way in ((0, "y"), (0, "r"), (1, "l"), (1, "y"), (1, "r"), (0, "l")):
        tok.send(0, 0, half, way)
    win.send(0, 0, "s")
    for copy in loads[3:]:
        copy.wait()
    mine = yo.at[2 * yh + yl]
    for i, dev in enumerate((beside, across, corner)):
        push(mine, mine, ys.at[i], yr.at[i], dev)

    acc[...] = jnp.zeros_like(acc)
    ss[...] = jnp.zeros_like(ss)

    def norm(plane, dx):
        slot = tok.slot(plane, dx)
        rows3 = xg[slot, ROWS:XROWS, :].astype(F32)
        g = rows3[0:1] + rows3[1:2] + rows3[2:3]

        @pl.loop(0, NB)
        def _(b):
            rows = pl.ds(pl.multiple_of(b * BLK, BLK), BLK)
            t = xg[slot, rows, :].astype(F32)
            sq = t * t
            ss[rows, :] += (sq[:, 0:128] + sq[:, 128:256]) + (sq[:, 256:384] + sq[:, 384:512])
            a = (t * g).astype(BF)
            ag[2 * slot, rows, :] = a[:, 0:256]
            ag[2 * slot + 1, rows, :] = a[:, 256:512]

    def spread_filters():
        ext[:, 0:BLK] = filt_v[...].astype(F32)
        ext[:, BLK:] = jnp.zeros((ext.shape[0], BLK), F32)

        @pl.loop(0, ext.shape[0])
        def _(g):
            row_ = jnp.broadcast_to(ext[pl.ds(g, 1), :], (2 * BLK, 2 * BLK))
            shifted = pltpu.roll(row_, BLK, 1, stride=1, stride_axis=0)
            toep[pl.ds(pl.multiple_of(g * BLK, BLK), BLK), :] = shifted[:, 0:BLK].T.astype(BF)

    opposite = tok.slot(0, 2)
    opposite_there = tok.slot(1, 2)

    def project(count, q_of, when):
        @pl.loop(0, count)
        def _(k):
            q = q_of(k)

            @pl.when(when(q))
            def _():
                @pl.loop(0, 3)
                def _(s):
                    acc[s, 8 : 8 + ROWS, :] += jnp.dot(ag[q], wg[q, s], preferred_element_type=F32)

    norm(0, 0)
    win.hop(0, 1)
    win.wait(1, 0)
    win.send(1, 0, "s")
    spread_filters()
    win.hop(0, 2)
    tok.wait(1, 0, 0)
    tok.send(1, 0, 0, "r")
    tok.wait(1, 0, 1)
    tok.send(1, 0, 1, "l")
    tok.send(1, 0, 1, "r")
    tok.send(1, 0, 0, "l")
    win.hop(0, 3)
    win.start(1)
    for dx in (NX - 1, 1):
        tok.wait(0, dx, 0)
        tok.wait(0, dx, 1)
        norm(0, dx)
    norm(1, 0)
    win.last(0)
    tok.wait(1, NX - 1, 0)
    tok.send(1, NX - 1, 0, "r")
    tok.wait(1, 1, 1)
    tok.send(1, 1, 1, "l")
    for i, (l_, h_) in enumerate(((1 - yl, yh), (yl, 1 - yh), (1 - yl, 1 - yh))):
        arrived(yo.at[2 * h_ + l_], ys.at[i], yr.at[i])
    for plane in range(NY):
        wo[plane, z, my_rows, :] = yo[2 * plane + yh]
    win.hop(1, 1)
    tok.send(0, NX - 1, 0, "r")
    tok.send(0, 1, 1, "l")
    for plane in range(NY):
        wout.start(plane)
        wout.send(plane, 0, "s")
    tok.wait(1, NX - 1, 1)
    norm(1, NX - 1)
    tok.wait(1, 1, 0)
    norm(1, 1)
    for dz in range(NZ):
        win.wait_sib(0, dz)
    project(
        8, lambda k: yl * NZ + k,
        lambda q: jnp.logical_and(q // 2 != opposite, q // 2 != opposite_there),
    )
    for dz in (5, 3):
        win.wait(1, dz)
        win.send(1, dz, "s")
    win.hop(1, 2)
    for plane in range(NY):
        wout.hop(plane, 1)
    tok.wait(1, 2, 0)
    tok.wait(1, 2, 1)
    norm(1, 2)
    project(2, lambda k: 2 * opposite_there + k, lambda q: yh != yl)
    for dz in (0, 1, 7, 2, 6, 5, 3):
        win.wait_sib(1, dz)
    project(
        7, lambda k: (1 - yl) * NZ + (z + k + (k > 3).astype(jnp.int32)) % NZ,
        lambda q: q // 2 != opposite,
    )
    win.wait(1, 4)
    win.send(1, 4, "s")
    tok.wait(0, 2, 0)
    tok.wait(0, 2, 1)
    norm(0, 2)
    project(2, lambda k: 2 * opposite + k, lambda q: q != (1 - yl) * NZ + (z + 4) % NZ)
    for plane in range(NY):
        wout.hop(plane, 2)
    win.wait_sib(1, 4)
    project(1, lambda k: (1 - yl) * NZ + (z + 4) % NZ, lambda q: q >= 0)

    lanes_group = lax.broadcasted_iota(jnp.int32, (BLK, 128), 1) // GSIZE

    def taps(s, b, j):
        cols = slice(128 * j, 128 * (j + 1))
        v = acc[s, pl.ds(pl.multiple_of(b * BLK, BLK), BLK + 8), cols]
        total = short_v[0, s : s + 1, cols] * v
        total = total + short_v[1, s : s + 1, cols] * pltpu.roll(v, 1, 0)
        total = total + short_v[2, s : s + 1, cols] * pltpu.roll(v, 2, 0)
        return total[8:]

    def settle(b):
        rows = pl.ds(pl.multiple_of(b * BLK, BLK), BLK)
        scale = lax.rsqrt(jnp.sum(ss[rows, :], axis=1, keepdims=True) / D + EPS)
        at_ = pl.ds(pl.multiple_of(b * BLK + 8, 8), BLK)
        for s in range(3):
            acc[s, at_, :] = (acc[s, at_, :] * scale).astype(BF).astype(F32)

    def gate(b):
        for j in range(4):
            kv = taps(1, b, j) * taps(2, b, j)
            gated[pl.ds(pl.multiple_of((b + 1) * BLK, BLK), BLK), 128 * j : 128 * (j + 1)] = kv.astype(BF)

    def combine(b):
        rows = pl.ds(pl.multiple_of(b * BLK, BLK), BLK)
        for j in range(4):
            cols = slice(128 * j, 128 * (j + 1))
            window = gated[pl.ds(pl.multiple_of(b * BLK, BLK), 2 * BLK), cols]
            every = jnp.dot(toep[1024 * j : 1024 * (j + 1), :], window, preferred_element_type=F32)
            medium = every[0:BLK]
            for g in range(1, 8):
                medium = jnp.where(lanes_group == g, every[BLK * g : BLK * (g + 1)], medium)
            direct = window[BLK:].astype(F32)
            mixed = taps(0, b, j) * (medium + skip_v[:, cols] * direct)
            mx[x, rows, cols] = mixed.astype(BF)

    halo_g = (gated.at[pl.ds(ROWS, BLK), :], gated.at[pl.ds(0, BLK), :])

    def halo_out():
        for s in range(3):
            hs_send[s] = acc[s, ROWS - 8 : ROWS + 8, :].astype(BF)
        push(hs_send, hs_recv, hs.at[0], hr.at[0], after)
        push(halo_g[0], halo_g[1], hs.at[1], hr.at[1], after)

    def halo_in():
        arrived(hs_recv, hs.at[0], hr.at[0])
        arrived(halo_g[1], hs.at[1], hr.at[1])
        inside = ctx > 0
        for s in range(3):
            acc[s, 0:8, :] = jnp.where(inside, hs_recv[s].astype(F32)[8:16], 0.0)
        gated[0:BLK, :] = jnp.where(inside, gated[0:BLK, :].astype(F32), 0.0).astype(BF)

    def give(b):
        for way in ("r", "l") if b % 2 else ("l", "r"):
            mix.send(0, 0, b, way)

    def relay(b):
        mix.wait(0, NX - 1, b)
        mix.send(0, NX - 1, b, "r")
        mix.wait(0, 1, b - 1)
        mix.send(0, 1, b - 1, "l")

    settle(5)
    settle(4)
    gate(5)
    halo_out()
    settle(3)
    gate(4)
    combine(5)
    give(5)
    settle(2)
    gate(3)
    combine(4)
    give(4)
    settle(1)
    gate(2)
    combine(3)
    settle(0)
    gate(1)
    combine(2)
    halo_in()
    gate(0)
    combine(1)
    combine(0)
    relay(5)
    give(3)
    give(2)
    for plane in range(NY):
        wout.hop(plane, 3)

    def product(plane, c):
        total = None
        for x_ in range(NX):
            w = wo[plane, 2 * x_ : 2 * x_ + 2].reshape(COLS, COLS)
            term = jnp.dot(mx[x_, CHUNK * c : CHUNK * (c + 1), :], w, preferred_element_type=F32)
            total = term if total is None else total + term
        return total

    def outward(c):
        b = 2 * c + 1
        for dx, piece in ((NX - 1, b - 1), (1, b), (2, b), (2, b - 1)):
            mix.wait(0, dx, piece)
        rows = slice(CHUNK * c, CHUNK * (c + 1))
        part_send[rows, :] = product(1 - yh, c).astype(BF)
        there = pl.ds(CHUNK * c, CHUNK)
        push(part_send.at[there, :], part_recv.at[there, :], ps.at[c], pr.at[c], across)
        acc2[rows, :] = xg[own, rows, :].astype(F32) + product(yh, c)

    def finish(c):
        there = pl.ds(CHUNK * c, CHUNK)
        rows = slice(CHUNK * c, CHUNK * (c + 1))
        arrived(part_recv.at[there, :], ps.at[c], pr.at[c])
        out_v[rows, :] = (acc2[rows, :] + part_recv[rows, :].astype(F32)).astype(BF)
        copy = pltpu.make_async_copy(out_v.at[there, :], out_ref.at[there, :], ls.at[c])
        copy.start()
        return copy

    relay(3)
    give(1)
    give(0)
    for plane in range(NY):
        wout.last(plane)
    for plane in range(NY):
        for dz in range(1, NZ):
            wout.wait_sib(plane, dz)
        wout.wait_sib(plane, 0)
    outward(2)
    relay(1)
    outward(1)
    outward(0)
    stores = [finish(2), finish(1), finish(0)]
    for copy in stores:
        copy.wait()
    for copy in sends:
        copy.wait_send()


def body(tokens, norm_gain, in_weight, short_weight, filters, skip, out_weight):
    dma = pltpu.SemaphoreType.DMA
    hbm = pl.BlockSpec(memory_space=pl.ANY)
    return pl.pallas_call(
        kernel,
        out_shape=jax.ShapeDtypeStruct((ROWS, COLS), BF),
        in_specs=[hbm] * 7,
        out_specs=hbm,
        scratch_shapes=[
            pltpu.VMEM((8, XROWS, COLS), BF),
            pltpu.VMEM((16, ROWS, 2 * DEPTH), BF),
            pltpu.VMEM((16, 3, 2 * DEPTH, COLS), BF),
            pltpu.VMEM((2, NZ, 2 * DEPTH, COLS), BF),
            pltpu.VMEM((4, DEPTH, COLS), BF),
            pltpu.VMEM((4, ROWS, COLS), BF),
            pltpu.VMEM((3, ROWS + 8, COLS), F32),
            pltpu.VMEM((ROWS, COLS), F32),
            pltpu.VMEM((ROWS + BLK, COLS), BF),
            pltpu.VMEM((32 * BLK, 2 * BLK), BF),
            pltpu.VMEM((32, 2 * BLK), F32),
            pltpu.VMEM((ROWS, 128), F32),
            pltpu.VMEM((3, 16, COLS), BF),
            pltpu.VMEM((3, 16, COLS), BF),
            pltpu.VMEM((ROWS, COLS), BF),
            pltpu.VMEM((ROWS, COLS), BF),
            pltpu.VMEM((ROWS, COLS), BF),
            pltpu.VMEM((1, COLS), F32),
            pltpu.VMEM((3, 3, COLS), F32),
            pltpu.VMEM((32, BLK), BF),
            pltpu.VMEM((1, COLS), F32),
            dma((7,)),
            dma((14,)), dma((2, 4, 2)),
            dma((18,)), dma((1, 4, 6)),
            dma((50,)), dma((2, 8, 2)), dma((2, 8)),
            dma((60,)), dma((2, 8, 2)), dma((2, 8)),
            dma((3,)), dma((3,)),
            dma((3,)), dma((3,)),
            dma((2,)), dma((2,)),
        ],
        compiler_params=pltpu.CompilerParams(
            collective_id=0, has_side_effects=True, vmem_limit_bytes=58 * 1024 * 1024
        ),
    )(
        tokens,
        norm_gain.reshape(1, COLS),
        jnp.transpose(in_weight, (1, 0, 2)),
        short_weight,
        filters.T,
        skip.reshape(1, COLS),
        out_weight,
    )


def solution(mesh):
    return jax.shard_map(
        body,
        mesh=mesh,
        in_specs=(
            P("ctx", "mp"),
            P("mp"),
            P("ctx", None, "mp"),
            P(None, None, "mp"),
            P(None, "mp"),
            P("mp"),
            P("ctx", "mp"),
        ),
        out_specs=P("ctx", "mp"),
        check_vma=False,
    )
```

```python
import jax
import jax.numpy as jnp
from jax import lax
from jax.experimental import pallas as pl
from jax.experimental.pallas import tpu as pltpu
from jax.sharding import PartitionSpec as P

D = 4096
EPS = 1e-06
NX, NZ, NY = 4, 8, 2
ROWS, COLS, DEPTH = 768, 512, 128
BLK = 128
NB = ROWS // BLK
XROWS = ROWS + 16
HALF = 384
GSIZE = 16
FAR = NZ // 2
PIECES = ((640, 128), (512, 128), (384, 128), (256, 128), (192, 64), (128, 64), (64, 64), (0, 64))
CHUNKS = ((512, 256), (256, 256), (128, 128), (0, 128))
BF = jnp.bfloat16
F32 = jnp.float32


def kernel(
    tok_ref, gain_ref, inw_ref, short_ref, filt_ref, skip_ref, outw_ref,
    out_ref,
    xg, ag, wg, wo, yo, mx, acc, acc2, gated, toep, ext, ss, hs_send, hs_recv,
    part_send, part_recv, out_v, gain_v, short_v, filt_v, skip_v,
    ls, xs, xr, ms, mr, wsend, wrecv, wsib, osend, orecv, osib, ys, yr, ps, pr, hs, hr,
):
    ctx = lax.axis_index("ctx")
    mp = lax.axis_index("mp")
    core = ctx % 2
    z = (ctx // 2) % NZ
    yl = ctx // (2 * NZ)
    x = mp % NX
    yh = mp // NX

    def at(yl_, z_, core_, yh_, x_):
        return ((yl_ * NZ + z_) * 2 + core_, yh_ * NX + x_)

    right = at(yl, z, core, yh, (x + 1) % NX)
    left = at(yl, z, core, yh, (x + NX - 1) % NX)
    across = at(yl, z, core, 1 - yh, x)
    up = at(yl, (z + 1) % NZ, core, yh, x)
    down = at(yl, (z + NZ - 1) % NZ, core, yh, x)
    beside = at(1 - yl, z, core, yh, x)
    corner = at(1 - yl, z, core, 1 - yh, x)
    sib = at(yl, z, 1 - core, yh, x)
    after = ((ctx + 1) % (4 * NZ), mp)
    before = ((ctx + 4 * NZ - 1) % (4 * NZ), mp)

    barrier = pltpu.get_barrier_semaphore()
    everyone = (right, left, across, up, down, beside, corner, sib, after, before)
    for dev in everyone:
        pl.semaphore_signal(barrier, inc=1, device_id=dev, device_id_type=pl.DeviceIdType.MESH)

    own = mp
    row = yl * NZ + z
    my_rows = pl.ds(pl.multiple_of(core * DEPTH, DEPTH), DEPTH)
    loads = [
        pltpu.make_async_copy(src, dst, ls.at[i])
        for i, (src, dst) in enumerate((
            (inw_ref, wg.at[row, :, my_rows, :]),
            (tok_ref, xg.at[own, pl.ds(0, ROWS), :]),
            (gain_ref, gain_v),
            (outw_ref, yo.at[0]),
            (filt_ref, filt_v),
            (short_ref, short_v),
            (skip_ref, skip_v),
        ))
    ]
    for copy in loads:
        copy.start()

    loads[2].wait()
    gain = gain_v[...]
    g_hi = gain.astype(BF).astype(F32)
    g_mid = (gain - g_hi).astype(BF).astype(F32)
    g_lo = gain - g_hi - g_mid
    which = lax.broadcasted_iota(jnp.int32, (16, COLS), 0)
    parts = jnp.where(which == 0, g_hi, jnp.where(which == 1, g_mid, jnp.where(which == 2, g_lo, 0.0)))
    xg[own, ROWS:XROWS, :] = parts.astype(BF)
    loads[0].wait()
    loads[1].wait()

    pl.semaphore_wait(barrier, len(everyone))

    sends = []

    def push(src, dst, ssem, rsem, dev):
        copy = pltpu.make_async_remote_copy(
            src_ref=src, dst_ref=dst, send_sem=ssem, recv_sem=rsem,
            device_id=dev, device_id_type=pl.DeviceIdType.MESH,
        )
        copy.start()
        sends.append(copy)

    def arrived(dst, ssem, rsem):
        pltpu.make_async_remote_copy(
            src_ref=dst, dst_ref=dst, send_sem=ssem, recv_sem=rsem,
            device_id=sib, device_id_type=pl.DeviceIdType.MESH,
        ).wait_recv()

    class Ring:
        def __init__(self, buf, planes, ssem, rsem, pieces):
            self.buf, self.planes = buf, planes
            self.ssem, self.rsem, self.pieces = ssem, rsem, pieces
            self.count = 0

        def slot(self, plane, dx):
            return ((yh + plane) % NY if self.planes == 2 else 0) * NX + (x + dx) % NX

        def view(self, plane, dx, piece):
            begin, size = self.pieces[piece]
            return self.buf.at[self.slot(plane, dx), pl.ds(begin, size), :]

        def send(self, plane, dx, piece, way):
            dev, shift = {"r": (right, 1), "l": (left, NX - 1), "y": (across, 0)}[way]
            there = (1, 0) if way == "y" else (plane, (dx + NX - shift) % NX)
            view = self.view(plane, dx, piece)
            push(
                view, view, self.ssem.at[self.count],
                self.rsem.at[there[0], there[1], piece], dev,
            )
            self.count += 1

        def wait(self, plane, dx, piece):
            arrived(self.view(plane, dx, piece), self.ssem.at[0], self.rsem.at[plane, dx, piece])

    class Column:
        def __init__(self, view_of, ssem, rsem, sibsem):
            self.view_of = view_of
            self.ssem, self.rsem, self.sibsem = ssem, rsem, sibsem
            self.count = 0

        def view(self, plane, dz, parity, part=None):
            begin, size = parity * DEPTH, DEPTH
            if part is not None:
                begin, size = begin + part * (DEPTH // 2), DEPTH // 2
            return self.view_of(plane, (z + dz) % NZ, pl.ds(begin, size))

        def send(self, plane, dz, way, part=None):
            dev, shift = {"u": (up, 1), "d": (down, NZ - 1), "y": (beside, 0), "s": (sib, 0)}[way]
            view = self.view(plane, dz, core, part)
            if way == "s":
                rsem = self.sibsem.at[plane, dz]
            elif way == "y":
                rsem = self.rsem.at[1, dz, part or 0]
            else:
                rsem = self.rsem.at[plane, (dz + NZ - shift) % NZ, part]
            push(view, view, self.ssem.at[self.count], rsem, dev)
            self.count += 1

        def wait(self, plane, dz, part=None):
            arrived(
                self.view(plane, dz, core, part), self.ssem.at[0],
                self.rsem.at[plane, dz, 0 if part is None else part],
            )

        def wait_sib(self, plane, dz):
            arrived(self.view(plane, dz, 1 - core), self.ssem.at[0], self.sibsem.at[plane, dz])

        def start(self, plane):
            for part in (0, 1):
                self.send(plane, 0, "u", part)
                self.send(plane, 0, "d", 1 - part)

        def hop(self, plane, dist):
            end = FAR - 1 if plane == 1 else FAR
            for turn in (0, 1):
                for dz, way, part in ((NZ - dist, "u", turn), (dist, "d", 1 - turn)):
                    self.wait(plane, dz, part)
                    if dist + 1 < end or dist + 1 == end and turn == 0:
                        self.send(plane, dz, way, part)
                    if plane == 0 and dist == FAR - 1 and turn == 1:
                        self.send(plane, dz, "y", part)
            for dz in (NZ - dist, dist):
                self.send(plane, dz, "s")

        def last(self, plane):
            self.wait(plane, FAR, 0)
            self.wait(plane, FAR, 1)
            if plane == 0:
                self.send(0, FAR, "y")
            self.send(plane, FAR, "s")

    tok = Ring(xg, 2, xs, xr, ((0, HALF), (HALF, XROWS - HALF)))
    mix = Ring(mx, 1, ms, mr, PIECES)
    win = Column(
        lambda plane, z_, rows: wg.at[((yl + plane) % NY) * NZ + z_, :, rows, :],
        wsend, wrecv, wsib,
    )
    wout = Column(
        lambda plane, z_, rows: wo.at[(yl + plane) % NY, z_, rows, :],
        osend, orecv, osib,
    )

    tok.send(0, 0, 0, "y")
    win.start(0)
    for half, way in ((0, "r"), (1, "l"), (1, "y"), (1, "r"), (0, "l")):
        tok.send(0, 0, half, way)
    win.send(0, 0, "s")
    for copy in loads[3:]:
        copy.wait()

    acc[...] = jnp.zeros_like(acc)
    ss[...] = jnp.zeros_like(ss)

    def norm(plane, dx):
        slot = tok.slot(plane, dx)
        rows3 = xg[slot, ROWS:XROWS, :].astype(F32)
        g = rows3[0:1] + rows3[1:2] + rows3[2:3]

        @pl.loop(0, NB)
        def _(b):
            rows = pl.ds(pl.multiple_of(b * BLK, BLK), BLK)
            t = xg[slot, rows, :].astype(F32)
            sq = t * t
            ss[rows, :] += (sq[:, 0:128] + sq[:, 128:256]) + (sq[:, 256:384] + sq[:, 384:512])
            a = (t * g).astype(BF)
            ag[2 * slot, rows, :] = a[:, 0:256]
            ag[2 * slot + 1, rows, :] = a[:, 256:512]

    def spread_filters(piece):
        if piece == 0:
            ext[:, 0:BLK] = filt_v[...].astype(F32)
            ext[:, BLK:] = jnp.zeros((ext.shape[0], BLK), F32)

        @pl.loop(8 * piece, 8 * piece + 8)
        def _(g):
            row_ = jnp.broadcast_to(ext[pl.ds(g, 1), :], (2 * BLK, 2 * BLK))
            shifted = pltpu.roll(row_, BLK, 1, stride=1, stride_axis=0)
            toep[pl.ds(pl.multiple_of(g * BLK, BLK), BLK), :] = shifted[:, 0:BLK].T.astype(BF)

    opposite = tok.slot(0, 2)
    opposite_there = tok.slot(1, 2)

    def project(count, q_of, when, begin=0, size=ROWS):
        rows = slice(begin, begin + size)

        @pl.loop(0, count)
        def _(k):
            q = q_of(k)

            @pl.when(when(q))
            def _():
                @pl.loop(0, 3)
                def _(s):
                    acc[s, 8 + begin : 8 + begin + size, :] += jnp.dot(
                        ag[q, rows], wg[q, s], preferred_element_type=F32
                    )

    def project_pair(count, slot_of, when, begin=0, size=ROWS):
        rows = slice(begin, begin + size)

        @pl.loop(0, count)
        def _(k):
            q = 2 * slot_of(k)

            @pl.when(when(slot_of(k)))
            def _():
                a = jnp.concatenate([ag[q, rows], ag[q + 1, rows]], axis=1)

                @pl.loop(0, 3)
                def _(s):
                    w = jnp.concatenate([wg[q, s], wg[q + 1, s]], axis=0)
                    acc[s, 8 + begin : 8 + begin + size, :] += jnp.dot(a, w, preferred_element_type=F32)

    norm(0, 0)
    win.hop(0, 1)
    win.send(0, 0, "y")
    tok.wait(1, 0, 0)
    tok.send(1, 0, 0, "r")
    tok.send(1, 0, 0, "l")
    spread_filters(0)
    win.hop(0, 2)
    tok.wait(1, 0, 1)
    tok.send(1, 0, 1, "l")
    tok.send(1, 0, 1, "r")
    push(yo.at[0], yo.at[1], ys.at[0], yr.at[0], corner)
    for dx in (NX - 1, 1):
        tok.wait(0, dx, 0)
        tok.wait(0, dx, 1)
        norm(0, dx)
    norm(1, 0)
    spread_filters(1)
    win.hop(0, 3)
    win.wait(1, 0)
    win.start(1)
    win.send(1, 0, "s")
    tok.wait(1, NX - 1, 0)
    tok.send(1, NX - 1, 0, "r")
    tok.send(0, NX - 1, 0, "r")
    spread_filters(2)
    win.last(0)
    for dz in range(NZ):
        win.wait_sib(0, dz)
    beyond = [tok.slot(1, NX - 1), tok.slot(1, 1)]

    def early(slot):
        ok = jnp.logical_and(slot != opposite, slot != opposite_there)
        return jnp.logical_and(ok, jnp.logical_and(slot != beyond[0], slot != beyond[1]))

    project_pair(4, lambda k: yl * (NZ // 2) + k, early)
    tok.wait(1, 1, 0)
    tok.wait(1, 1, 1)
    tok.send(1, 1, 1, "l")
    tok.send(0, 1, 1, "l")
    win.hop(1, 1)
    norm(1, 1)
    tok.wait(1, NX - 1, 1)
    norm(1, NX - 1)
    arrived(yo.at[1], ys.at[0], yr.at[0])
    wo[yl, z, my_rows, :] = jnp.where(yl == yh, yo[0], yo[1])
    wout.send(0, 0, "y")
    spread_filters(3)
    project_pair(2, lambda k: (1 - yh) * NX + (x + 1 + 2 * k) % NX, lambda slot: yh != yl)
    for dz in (0, 1, 7):
        win.wait_sib(1, dz)

    def there(k):
        return (1 - yl) * NZ + (z + NZ - 1 + k) % NZ

    project(
        3, there, lambda q: jnp.logical_and(q // 2 != opposite, q // 2 != opposite_there)
    )
    win.hop(1, 2)
    wout.start(0)
    wout.send(0, 0, "s")
    tok.wait(1, 2, 0)
    tok.wait(1, 2, 1)
    norm(1, 2)
    project_pair(1, lambda k: opposite_there, lambda slot: yh != yl)
    project(
        3, there, lambda q: jnp.logical_and(q // 2 == opposite_there, yh == yl)
    )
    win.wait(1, FAR)
    win.send(1, FAR, "s")
    win.wait_sib(1, 2)
    win.wait_sib(1, 6)
    project(
        2, lambda k: (1 - yl) * NZ + (z + 2 + 4 * k) % NZ, lambda q: q // 2 != opposite
    )
    wout.wait(1, 0)
    wout.start(1)
    wout.send(1, 0, "s")
    for dz in (5, 3):
        win.wait(1, dz, 0)
        win.wait(1, dz, 1)
        win.send(1, dz, "s")
    win.wait_sib(1, FAR)
    project(1, lambda k: (1 - yl) * NZ + (z + FAR) % NZ, lambda q: q // 2 != opposite)
    tok.wait(0, 2, 0)
    tok.wait(0, 2, 1)
    norm(0, 2)
    win.wait_sib(1, 5)
    win.wait_sib(1, 3)

    last_up = (1 - yl) * NZ + (z + FAR + 1) % NZ
    last_down = (1 - yl) * NZ + (z + FAR - 1) % NZ

    def final(begin, size):
        rows = slice(begin, begin + size)
        pieces = [ag[2 * opposite, rows], ag[2 * opposite + 1, rows]]
        for q in (last_up, last_down):
            a = ag[q, rows]
            pieces.append(jnp.where(q // 2 != opposite, a, jnp.zeros_like(a)))
        a = jnp.concatenate(pieces, axis=1)
        scale = lax.rsqrt(jnp.sum(ss[rows, :], axis=1, keepdims=True) / D + EPS)

        @pl.loop(0, 3)
        def _(s):
            w = jnp.concatenate(
                [wg[2 * opposite, s], wg[2 * opposite + 1, s], wg[last_up, s], wg[last_down, s]], axis=0
            )
            there = slice(8 + begin, 8 + begin + size)
            total = acc[s, there, :] + jnp.dot(a, w, preferred_element_type=F32)
            acc[s, there, :] = (total * scale).astype(BF).astype(F32)

    lanes_group = lax.broadcasted_iota(jnp.int32, (BLK, 128), 1) // GSIZE

    def taps(s, b, j):
        cols = slice(128 * j, 128 * (j + 1))
        v = acc[s, pl.ds(pl.multiple_of(b * BLK, BLK), BLK + 8), cols]
        total = short_v[0, s : s + 1, cols] * v
        total = total + short_v[1, s : s + 1, cols] * pltpu.roll(v, 1, 0)
        total = total + short_v[2, s : s + 1, cols] * pltpu.roll(v, 2, 0)
        return total[8:]

    def gate(b):
        for j in range(4):
            kv = taps(1, b, j) * taps(2, b, j)
            gated[pl.ds(pl.multiple_of((b + 1) * BLK, BLK), BLK), 128 * j : 128 * (j + 1)] = kv.astype(BF)

    def combine(b):
        rows = pl.ds(pl.multiple_of(b * BLK, BLK), BLK)
        for j in range(4):
            cols = slice(128 * j, 128 * (j + 1))
            window = gated[pl.ds(pl.multiple_of(b * BLK, BLK), 2 * BLK), cols]
            every = jnp.dot(toep[1024 * j : 1024 * (j + 1), :], window, preferred_element_type=F32)
            medium = every[0:BLK]
            for g in range(1, 8):
                medium = jnp.where(lanes_group == g, every[BLK * g : BLK * (g + 1)], medium)
            direct = window[BLK:].astype(F32)
            mixed = taps(0, b, j) * (medium + skip_v[:, cols] * direct)
            mx[x, rows, cols] = mixed.astype(BF)

    halo_g = (gated.at[pl.ds(ROWS, BLK), :], gated.at[pl.ds(0, BLK), :])

    def halo_out():
        for s in range(3):
            hs_send[s] = acc[s, ROWS - 8 : ROWS + 8, :].astype(BF)
        push(hs_send, hs_recv, hs.at[0], hr.at[0], after)
        push(halo_g[0], halo_g[1], hs.at[1], hr.at[1], after)

    def halo_in():
        arrived(hs_recv, hs.at[0], hr.at[0])
        arrived(halo_g[1], hs.at[1], hr.at[1])
        inside = ctx > 0
        for s in range(3):
            acc[s, 0:8, :] = jnp.where(inside, hs_recv[s].astype(F32)[8:16], 0.0)
        gated[0:BLK, :] = jnp.where(inside, gated[0:BLK, :].astype(F32), 0.0).astype(BF)

    def give(c):
        for piece, way in ((2 * c, "r"), (2 * c + 1, "l"), (2 * c + 1, "r"), (2 * c, "l")):
            mix.send(0, 0, piece, way)

    def relay(c):
        mix.wait(0, NX - 1, 2 * c)
        mix.send(0, NX - 1, 2 * c, "r")
        mix.wait(0, 1, 2 * c + 1)
        mix.send(0, 1, 2 * c + 1, "l")

    final(HALF, HALF)
    wout.hop(0, 1)
    gate(5)
    halo_out()
    gate(4)
    combine(5)
    mix.send(0, 0, 0, "r")
    mix.send(0, 0, 0, "l")
    wout.hop(0, 2)
    final(0, HALF)
    gate(3)
    combine(4)
    mix.send(0, 0, 1, "l")
    mix.send(0, 0, 1, "r")
    wout.hop(0, 3)
    wout.hop(1, 1)
    gate(2)
    combine(3)
    gate(1)
    combine(2)
    relay(0)
    give(1)
    wout.last(0)
    halo_in()
    gate(0)
    combine(1)
    combine(0)
    wout.hop(1, 2)
    relay(1)
    give(2)
    give(3)
    for dz in (5, 3):
        wout.wait(1, dz, 0)
        wout.wait(1, dz, 1)
        wout.send(1, dz, "s")
    wout.wait(1, FAR)
    wout.send(1, FAR, "s")

    def product(plane, rows):
        total = None
        for x_ in range(NX):
            w = wo[plane, 2 * x_ : 2 * x_ + 2].reshape(COLS, COLS)
            term = jnp.dot(mx[x_, rows, :], w, preferred_element_type=F32)
            total = term if total is None else total + term
        return total

    def theirs(c):
        for dx, piece in ((NX - 1, 2 * c + 1), (1, 2 * c), (2, 2 * c), (2, 2 * c + 1)):
            mix.wait(0, dx, piece)
        rows = slice(CHUNKS[c][0], sum(CHUNKS[c]))
        there = pl.ds(*CHUNKS[c])
        part_send[rows, :] = product(1 - yh, rows).astype(BF)
        push(part_send.at[there, :], part_recv.at[there, :], ps.at[c], pr.at[c], across)

    def ours(c):
        rows = slice(CHUNKS[c][0], sum(CHUNKS[c]))
        acc2[rows, :] = xg[own, rows, :].astype(F32) + product(yh, rows)

    def finish(c):
        rows = slice(CHUNKS[c][0], sum(CHUNKS[c]))
        there = pl.ds(*CHUNKS[c])
        arrived(part_recv.at[there, :], ps.at[c], pr.at[c])
        out_v[rows, :] = (acc2[rows, :] + part_recv[rows, :].astype(F32)).astype(BF)
        copy = pltpu.make_async_copy(out_v.at[there, :], out_ref.at[there, :], ls.at[c])
        copy.start()
        return copy

    for plane in range(NY):
        for dz in range(NZ):
            wout.wait_sib(plane, dz)
    theirs(0)
    relay(2)
    theirs(1)
    relay(3)
    ours(0)
    ours(1)
    theirs(2)
    theirs(3)
    ours(2)
    ours(3)
    stores = [finish(0), finish(1), finish(2), finish(3)]
    for copy in stores:
        copy.wait()
    for copy in sends:
        copy.wait_send()


def body(tokens, norm_gain, in_weight, short_weight, filters, skip, out_weight):
    dma = pltpu.SemaphoreType.DMA
    hbm = pl.BlockSpec(memory_space=pl.ANY)
    return pl.pallas_call(
        kernel,
        out_shape=jax.ShapeDtypeStruct((ROWS, COLS), BF),
        in_specs=[hbm] * 7,
        out_specs=hbm,
        scratch_shapes=[
            pltpu.VMEM((8, XROWS, COLS), BF),
            pltpu.VMEM((16, ROWS, 2 * DEPTH), BF),
            pltpu.VMEM((16, 3, 2 * DEPTH, COLS), BF),
            pltpu.VMEM((2, NZ, 2 * DEPTH, COLS), BF),
            pltpu.VMEM((2, DEPTH, COLS), BF),
            pltpu.VMEM((4, ROWS, COLS), BF),
            pltpu.VMEM((3, ROWS + 8, COLS), F32),
            pltpu.VMEM((ROWS, COLS), F32),
            pltpu.VMEM((ROWS + BLK, COLS), BF),
            pltpu.VMEM((32 * BLK, 2 * BLK), BF),
            pltpu.VMEM((32, 2 * BLK), F32),
            pltpu.VMEM((ROWS, 128), F32),
            pltpu.VMEM((3, 16, COLS), BF),
            pltpu.VMEM((3, 16, COLS), BF),
            pltpu.VMEM((ROWS, COLS), BF),
            pltpu.VMEM((ROWS, COLS), BF),
            pltpu.VMEM((ROWS, COLS), BF),
            pltpu.VMEM((1, COLS), F32),
            pltpu.VMEM((3, 3, COLS), F32),
            pltpu.VMEM((32, BLK), BF),
            pltpu.VMEM((1, COLS), F32),
            dma((7,)),
            dma((14,)), dma((2, 4, 2)),
            dma((24,)), dma((1, 4, 8)),
            dma((50,)), dma((2, 8, 2)), dma((2, 8)),
            dma((60,)), dma((2, 8, 2)), dma((2, 8)),
            dma((1,)), dma((1,)),
            dma((4,)), dma((4,)),
            dma((2,)), dma((2,)),
        ],
        compiler_params=pltpu.CompilerParams(
            collective_id=0, has_side_effects=True, vmem_limit_bytes=58 * 1024 * 1024
        ),
    )(
        tokens,
        norm_gain.reshape(1, COLS),
        jnp.transpose(in_weight, (1, 0, 2)),
        short_weight,
        filters.T,
        skip.reshape(1, COLS),
        out_weight,
    )


def solution(mesh):
    return jax.shard_map(
        body,
        mesh=mesh,
        in_specs=(
            P("ctx", "mp"),
            P("mp"),
            P("ctx", None, "mp"),
            P(None, None, "mp"),
            P(None, "mp"),
            P("mp"),
            P("ctx", "mp"),
        ),
        out_specs=P("ctx", "mp"),
        check_vma=False,
    )
```

```python
import jax
import jax.numpy as jnp
from jax import lax
from jax.experimental import pallas as pl
from jax.experimental.pallas import tpu as pltpu
from jax.sharding import PartitionSpec as P

D = 4096
EPS = 1e-06
NX, NZ, NY = 4, 8, 2
ROWS, COLS, DEPTH = 768, 512, 128
BLK = 128
NB = ROWS // BLK
XROWS = ROWS + 16
HALF = 384
GSIZE = 16
FAR = NZ // 2
PIECES = ((640, 128), (512, 128), (384, 128), (256, 128), (192, 64), (128, 64), (64, 64), (0, 64))
CHUNKS = ((512, 256), (256, 256), (128, 128), (0, 128))
BF = jnp.bfloat16
F32 = jnp.float32


def kernel(
    tok_ref, gain_ref, inw_ref, short_ref, filt_ref, skip_ref, outw_ref,
    out_ref,
    xg, ag, wg, wo, yo, mx, acc, acc2, gated, toep, ext, ss, hs_send, hs_recv,
    part_send, part_recv, out_v, gain_v, short_v, filt_v, skip_v,
    ls, xs, xr, ms, mr, wsend, wrecv, wsib, osend, orecv, osib, ys, yr, ps, pr, hs, hr,
):
    ctx = lax.axis_index("ctx")
    mp = lax.axis_index("mp")
    core = ctx % 2
    z = (ctx // 2) % NZ
    yl = ctx // (2 * NZ)
    x = mp % NX
    yh = mp // NX

    def at(yl_, z_, core_, yh_, x_):
        return ((yl_ * NZ + z_) * 2 + core_, yh_ * NX + x_)

    right = at(yl, z, core, yh, (x + 1) % NX)
    left = at(yl, z, core, yh, (x + NX - 1) % NX)
    across = at(yl, z, core, 1 - yh, x)
    up = at(yl, (z + 1) % NZ, core, yh, x)
    down = at(yl, (z + NZ - 1) % NZ, core, yh, x)
    beside = at(1 - yl, z, core, yh, x)
    corner = at(1 - yl, z, core, 1 - yh, x)
    sib = at(yl, z, 1 - core, yh, x)
    after = ((ctx + 1) % (4 * NZ), mp)
    before = ((ctx + 4 * NZ - 1) % (4 * NZ), mp)

    barrier = pltpu.get_barrier_semaphore()
    everyone = (right, left, across, up, down, beside, corner, sib, after, before)
    for dev in everyone:
        pl.semaphore_signal(barrier, inc=1, device_id=dev, device_id_type=pl.DeviceIdType.MESH)

    own = mp
    row = yl * NZ + z
    my_rows = pl.ds(pl.multiple_of(core * DEPTH, DEPTH), DEPTH)
    loads = [
        pltpu.make_async_copy(src, dst, ls.at[i])
        for i, (src, dst) in enumerate((
            (inw_ref, wg.at[row, :, my_rows, :]),
            (tok_ref, xg.at[own, pl.ds(0, ROWS), :]),
            (gain_ref, gain_v),
            (outw_ref, yo.at[0]),
            (filt_ref, filt_v),
            (short_ref, short_v),
            (skip_ref, skip_v),
        ))
    ]
    for copy in loads:
        copy.start()

    loads[2].wait()
    gain = gain_v[...]
    g_hi = gain.astype(BF).astype(F32)
    g_mid = (gain - g_hi).astype(BF).astype(F32)
    g_lo = gain - g_hi - g_mid
    which = lax.broadcasted_iota(jnp.int32, (16, COLS), 0)
    parts = jnp.where(which == 0, g_hi, jnp.where(which == 1, g_mid, jnp.where(which == 2, g_lo, 0.0)))
    xg[own, ROWS:XROWS, :] = parts.astype(BF)
    loads[0].wait()
    loads[1].wait()

    pl.semaphore_wait(barrier, len(everyone))

    sends = []

    def push(src, dst, ssem, rsem, dev):
        copy = pltpu.make_async_remote_copy(
            src_ref=src, dst_ref=dst, send_sem=ssem, recv_sem=rsem,
            device_id=dev, device_id_type=pl.DeviceIdType.MESH,
        )
        copy.start()
        sends.append(copy)

    def arrived(dst, ssem, rsem):
        pltpu.make_async_remote_copy(
            src_ref=dst, dst_ref=dst, send_sem=ssem, recv_sem=rsem,
            device_id=sib, device_id_type=pl.DeviceIdType.MESH,
        ).wait_recv()

    class Ring:
        def __init__(self, buf, planes, ssem, rsem, pieces):
            self.buf, self.planes = buf, planes
            self.ssem, self.rsem, self.pieces = ssem, rsem, pieces
            self.count = 0

        def slot(self, plane, dx):
            return ((yh + plane) % NY if self.planes == 2 else 0) * NX + (x + dx) % NX

        def view(self, plane, dx, piece):
            begin, size = self.pieces[piece]
            return self.buf.at[self.slot(plane, dx), pl.ds(begin, size), :]

        def send(self, plane, dx, piece, way):
            dev, shift = {"r": (right, 1), "l": (left, NX - 1), "y": (across, 0)}[way]
            there = (1, 0) if way == "y" else (plane, (dx + NX - shift) % NX)
            view = self.view(plane, dx, piece)
            push(
                view, view, self.ssem.at[self.count],
                self.rsem.at[there[0], there[1], piece], dev,
            )
            self.count += 1

        def wait(self, plane, dx, piece):
            arrived(self.view(plane, dx, piece), self.ssem.at[0], self.rsem.at[plane, dx, piece])

    class Column:
        def __init__(self, view_of, ssem, rsem, sibsem):
            self.view_of = view_of
            self.ssem, self.rsem, self.sibsem = ssem, rsem, sibsem
            self.count = 0

        def view(self, plane, dz, parity, part=None):
            begin, size = parity * DEPTH, DEPTH
            if part is not None:
                begin, size = begin + part * (DEPTH // 2), DEPTH // 2
            return self.view_of(plane, (z + dz) % NZ, pl.ds(begin, size))

        def send(self, plane, dz, way, part=None):
            dev, shift = {"u": (up, 1), "d": (down, NZ - 1), "y": (beside, 0), "s": (sib, 0)}[way]
            view = self.view(plane, dz, core, part)
            if way == "s":
                rsem = self.sibsem.at[plane, dz]
            elif way == "y":
                rsem = self.rsem.at[1, dz, part or 0]
            else:
                rsem = self.rsem.at[plane, (dz + NZ - shift) % NZ, part]
            push(view, view, self.ssem.at[self.count], rsem, dev)
            self.count += 1

        def wait(self, plane, dz, part=None):
            arrived(
                self.view(plane, dz, core, part), self.ssem.at[0],
                self.rsem.at[plane, dz, 0 if part is None else part],
            )

        def wait_sib(self, plane, dz):
            arrived(self.view(plane, dz, 1 - core), self.ssem.at[0], self.sibsem.at[plane, dz])

        def start(self, plane):
            for part in (0, 1):
                self.send(plane, 0, "u", part)
                self.send(plane, 0, "d", 1 - part)

        def hop(self, plane, dist):
            end = FAR - 1 if plane == 1 else FAR
            for turn in (0, 1):
                for dz, way, part in ((NZ - dist, "u", turn), (dist, "d", 1 - turn)):
                    self.wait(plane, dz, part)
                    if dist + 1 < end or dist + 1 == end and turn == 0:
                        self.send(plane, dz, way, part)
                    if plane == 0 and dist == FAR - 1 and turn == 1:
                        self.send(plane, dz, "y", part)
            for dz in (NZ - dist, dist):
                self.send(plane, dz, "s")

        def last(self, plane):
            self.wait(plane, FAR, 0)
            self.wait(plane, FAR, 1)
            if plane == 0:
                self.send(0, FAR, "y")
            self.send(plane, FAR, "s")

    tok = Ring(xg, 2, xs, xr, ((0, HALF), (HALF, XROWS - HALF)))
    mix = Ring(mx, 1, ms, mr, PIECES)
    win = Column(
        lambda plane, z_, rows: wg.at[((yl + plane) % NY) * NZ + z_, :, rows, :],
        wsend, wrecv, wsib,
    )
    wout = Column(
        lambda plane, z_, rows: wo.at[(yl + plane) % NY, z_, rows, :],
        osend, orecv, osib,
    )

    tok.send(0, 0, 0, "y")
    win.start(0)
    for half, way in ((0, "r"), (1, "l"), (1, "y"), (1, "r"), (0, "l")):
        tok.send(0, 0, half, way)
    win.send(0, 0, "s")
    for copy in loads[3:]:
        copy.wait()

    acc[...] = jnp.zeros_like(acc)
    ss[...] = jnp.zeros_like(ss)

    def norm(plane, dx):
        slot = tok.slot(plane, dx)
        rows3 = xg[slot, ROWS:XROWS, :].astype(F32)
        g = rows3[0:1] + rows3[1:2] + rows3[2:3]

        @pl.loop(0, NB)
        def _(b):
            rows = pl.ds(pl.multiple_of(b * BLK, BLK), BLK)
            t = xg[slot, rows, :].astype(F32)
            sq = t * t
            ss[rows, :] += (sq[:, 0:128] + sq[:, 128:256]) + (sq[:, 256:384] + sq[:, 384:512])
            a = (t * g).astype(BF)
            ag[2 * slot, rows, :] = a[:, 0:256]
            ag[2 * slot + 1, rows, :] = a[:, 256:512]

    def spread_filters(piece):
        if piece == 0:
            ext[:, 0:BLK] = filt_v[...].astype(F32)
            ext[:, BLK:] = jnp.zeros((ext.shape[0], BLK), F32)

        @pl.loop(8 * piece, 8 * piece + 8)
        def _(g):
            row_ = jnp.broadcast_to(ext[pl.ds(g, 1), :], (2 * BLK, 2 * BLK))
            shifted = pltpu.roll(row_, BLK, 1, stride=1, stride_axis=0)
            toep[pl.ds(pl.multiple_of(g * BLK, BLK), BLK), :] = shifted[:, 0:BLK].T.astype(BF)

    opposite = tok.slot(0, 2)
    opposite_there = tok.slot(1, 2)

    def project(count, q_of, when, begin=0, size=ROWS):
        rows = slice(begin, begin + size)

        @pl.loop(0, count)
        def _(k):
            q = q_of(k)

            @pl.when(when(q))
            def _():
                @pl.loop(0, 3)
                def _(s):
                    acc[s, 8 + begin : 8 + begin + size, :] += jnp.dot(
                        ag[q, rows], wg[q, s], preferred_element_type=F32
                    )

    def project_pair(count, slot_of, when, begin=0, size=ROWS):
        rows = slice(begin, begin + size)

        @pl.loop(0, count)
        def _(k):
            q = 2 * slot_of(k)

            @pl.when(when(slot_of(k)))
            def _():
                a = jnp.concatenate([ag[q, rows], ag[q + 1, rows]], axis=1)

                @pl.loop(0, 3)
                def _(s):
                    w = jnp.concatenate([wg[q, s], wg[q + 1, s]], axis=0)
                    acc[s, 8 + begin : 8 + begin + size, :] += jnp.dot(a, w, preferred_element_type=F32)

    norm(0, 0)
    win.hop(0, 1)
    win.send(0, 0, "y")
    tok.wait(1, 0, 0)
    tok.send(1, 0, 0, "r")
    tok.send(1, 0, 0, "l")
    spread_filters(0)
    win.hop(0, 2)
    tok.wait(1, 0, 1)
    tok.send(1, 0, 1, "l")
    tok.send(1, 0, 1, "r")
    push(yo.at[0], yo.at[1], ys.at[0], yr.at[0], corner)
    for dx in (NX - 1, 1):
        tok.wait(0, dx, 0)
        tok.wait(0, dx, 1)
        norm(0, dx)
    norm(1, 0)
    spread_filters(1)
    win.hop(0, 3)
    win.wait(1, 0)
    win.start(1)
    win.send(1, 0, "s")
    tok.wait(1, NX - 1, 0)
    tok.send(1, NX - 1, 0, "r")
    tok.send(0, NX - 1, 0, "r")
    spread_filters(2)
    win.last(0)
    for dz in range(NZ):
        win.wait_sib(0, dz)
    beyond = [tok.slot(1, NX - 1), tok.slot(1, 1)]

    def early(slot):
        ok = jnp.logical_and(slot != opposite, slot != opposite_there)
        return jnp.logical_and(ok, jnp.logical_and(slot != beyond[0], slot != beyond[1]))

    project_pair(4, lambda k: yl * (NZ // 2) + k, early)
    tok.wait(1, 1, 0)
    tok.wait(1, 1, 1)
    tok.send(1, 1, 1, "l")
    tok.send(0, 1, 1, "l")
    win.hop(1, 1)
    norm(1, 1)
    tok.wait(1, NX - 1, 1)
    norm(1, NX - 1)
    arrived(yo.at[1], ys.at[0], yr.at[0])
    wo[yl, z, my_rows, :] = jnp.where(yl == yh, yo[0], yo[1])
    wout.send(0, 0, "y")
    spread_filters(3)
    project_pair(2, lambda k: (1 - yh) * NX + (x + 1 + 2 * k) % NX, lambda slot: yh != yl)
    for dz in (0, 1, 7):
        win.wait_sib(1, dz)

    def there(k):
        return (1 - yl) * NZ + (z + NZ - 1 + k) % NZ

    project(
        3, there, lambda q: jnp.logical_and(q // 2 != opposite, q // 2 != opposite_there)
    )
    win.hop(1, 2)
    wout.start(0)
    wout.send(0, 0, "s")
    tok.wait(1, 2, 0)
    tok.wait(1, 2, 1)
    norm(1, 2)
    project_pair(1, lambda k: opposite_there, lambda slot: yh != yl)
    project(
        3, there, lambda q: jnp.logical_and(q // 2 == opposite_there, yh == yl)
    )
    win.wait(1, FAR)
    win.send(1, FAR, "s")
    win.wait_sib(1, 2)
    win.wait_sib(1, 6)
    project(
        2, lambda k: (1 - yl) * NZ + (z + 2 + 4 * k) % NZ, lambda q: q // 2 != opposite
    )
    wout.wait(1, 0)
    wout.start(1)
    wout.send(1, 0, "s")
    for dz in (5, 3):
        win.wait(1, dz, 0)
        win.wait(1, dz, 1)
        win.send(1, dz, "s")
    wout.hop(0, 1)
    win.wait_sib(1, FAR)
    project(1, lambda k: (1 - yl) * NZ + (z + FAR) % NZ, lambda q: q // 2 != opposite)
    tok.wait(0, 2, 0)
    tok.wait(0, 2, 1)
    norm(0, 2)
    win.wait_sib(1, 5)
    win.wait_sib(1, 3)

    last_up = (1 - yl) * NZ + (z + FAR + 1) % NZ
    last_down = (1 - yl) * NZ + (z + FAR - 1) % NZ

    def final(begin, size):
        rows = slice(begin, begin + size)
        pieces = [ag[2 * opposite, rows], ag[2 * opposite + 1, rows]]
        for q in (last_up, last_down):
            a = ag[q, rows]
            pieces.append(jnp.where(q // 2 != opposite, a, jnp.zeros_like(a)))
        a = jnp.concatenate(pieces, axis=1)
        scale = lax.rsqrt(jnp.sum(ss[rows, :], axis=1, keepdims=True) / D + EPS)

        @pl.loop(0, 3)
        def _(s):
            w = jnp.concatenate(
                [wg[2 * opposite, s], wg[2 * opposite + 1, s], wg[last_up, s], wg[last_down, s]], axis=0
            )
            there = slice(8 + begin, 8 + begin + size)
            total = acc[s, there, :] + jnp.dot(a, w, preferred_element_type=F32)
            acc[s, there, :] = (total * scale).astype(BF).astype(F32)

    lanes_group = lax.broadcasted_iota(jnp.int32, (BLK, 128), 1) // GSIZE

    def taps(s, b, j):
        cols = slice(128 * j, 128 * (j + 1))
        v = acc[s, pl.ds(pl.multiple_of(b * BLK, BLK), BLK + 8), cols]
        total = short_v[0, s : s + 1, cols] * v
        total = total + short_v[1, s : s + 1, cols] * pltpu.roll(v, 1, 0)
        total = total + short_v[2, s : s + 1, cols] * pltpu.roll(v, 2, 0)
        return total[8:]

    def gate(b):
        for j in range(4):
            kv = taps(1, b, j) * taps(2, b, j)
            gated[pl.ds(pl.multiple_of((b + 1) * BLK, BLK), BLK), 128 * j : 128 * (j + 1)] = kv.astype(BF)

    def combine(b):
        rows = pl.ds(pl.multiple_of(b * BLK, BLK), BLK)
        for j in range(4):
            cols = slice(128 * j, 128 * (j + 1))
            window = gated[pl.ds(pl.multiple_of(b * BLK, BLK), 2 * BLK), cols]
            every = jnp.dot(toep[1024 * j : 1024 * (j + 1), :], window, preferred_element_type=F32)
            medium = every[0:BLK]
            for g in range(1, 8):
                medium = jnp.where(lanes_group == g, every[BLK * g : BLK * (g + 1)], medium)
            direct = window[BLK:].astype(F32)
            mixed = taps(0, b, j) * (medium + skip_v[:, cols] * direct)
            mx[x, rows, cols] = mixed.astype(BF)

    halo_g = (gated.at[pl.ds(ROWS, BLK), :], gated.at[pl.ds(0, BLK), :])

    def halo_out():
        for s in range(3):
            hs_send[s] = acc[s, ROWS - 8 : ROWS + 8, :].astype(BF)
        push(hs_send, hs_recv, hs.at[0], hr.at[0], after)
        push(halo_g[0], halo_g[1], hs.at[1], hr.at[1], after)

    def halo_in():
        arrived(hs_recv, hs.at[0], hr.at[0])
        arrived(halo_g[1], hs.at[1], hr.at[1])
        inside = ctx > 0
        for s in range(3):
            acc[s, 0:8, :] = jnp.where(inside, hs_recv[s].astype(F32)[8:16], 0.0)
        gated[0:BLK, :] = jnp.where(inside, gated[0:BLK, :].astype(F32), 0.0).astype(BF)

    def give(c):
        for piece, way in ((2 * c, "r"), (2 * c + 1, "l"), (2 * c + 1, "r"), (2 * c, "l")):
            mix.send(0, 0, piece, way)

    def relay(c):
        mix.wait(0, NX - 1, 2 * c)
        mix.send(0, NX - 1, 2 * c, "r")
        mix.wait(0, 1, 2 * c + 1)
        mix.send(0, 1, 2 * c + 1, "l")

    final(HALF, HALF)
    gate(5)
    halo_out()
    gate(4)
    combine(5)
    mix.send(0, 0, 0, "r")
    mix.send(0, 0, 0, "l")
    wout.hop(0, 2)
    final(0, HALF)
    gate(3)
    combine(4)
    mix.send(0, 0, 1, "l")
    mix.send(0, 0, 1, "r")
    wout.hop(0, 3)
    wout.hop(1, 1)
    gate(2)
    combine(3)
    gate(1)
    combine(2)
    relay(0)
    give(1)
    wout.last(0)
    halo_in()
    gate(0)
    combine(1)
    combine(0)
    wout.hop(1, 2)
    for dz in (5, 3):
        wout.wait(1, dz, 0)
        wout.wait(1, dz, 1)
        wout.send(1, dz, "s")
    wout.wait(1, FAR)
    wout.send(1, FAR, "s")
    relay(1)
    give(2)
    give(3)

    def product(plane, rows):
        total = None
        for x_ in range(NX):
            w = wo[plane, 2 * x_ : 2 * x_ + 2].reshape(COLS, COLS)
            term = jnp.dot(mx[x_, rows, :], w, preferred_element_type=F32)
            total = term if total is None else total + term
        return total

    def theirs(c):
        for dx, piece in ((NX - 1, 2 * c + 1), (1, 2 * c), (2, 2 * c), (2, 2 * c + 1)):
            mix.wait(0, dx, piece)
        rows = slice(CHUNKS[c][0], sum(CHUNKS[c]))
        there = pl.ds(*CHUNKS[c])
        part_send[rows, :] = product(1 - yh, rows).astype(BF)
        push(part_send.at[there, :], part_recv.at[there, :], ps.at[c], pr.at[c], across)

    def ours(c):
        rows = slice(CHUNKS[c][0], sum(CHUNKS[c]))
        acc2[rows, :] = xg[own, rows, :].astype(F32) + product(yh, rows)

    def finish(c):
        rows = slice(CHUNKS[c][0], sum(CHUNKS[c]))
        there = pl.ds(*CHUNKS[c])
        arrived(part_recv.at[there, :], ps.at[c], pr.at[c])
        out_v[rows, :] = (acc2[rows, :] + part_recv[rows, :].astype(F32)).astype(BF)
        copy = pltpu.make_async_copy(out_v.at[there, :], out_ref.at[there, :], ls.at[c])
        copy.start()
        return copy

    for plane in range(NY):
        for dz in range(NZ):
            wout.wait_sib(plane, dz)
    theirs(0)
    relay(2)
    theirs(1)
    relay(3)
    ours(0)
    ours(1)
    theirs(2)
    theirs(3)
    ours(2)
    ours(3)
    stores = [finish(0), finish(1), finish(2), finish(3)]
    for copy in stores:
        copy.wait()
    for copy in sends:
        copy.wait_send()


def body(tokens, norm_gain, in_weight, short_weight, filters, skip, out_weight):
    dma = pltpu.SemaphoreType.DMA
    hbm = pl.BlockSpec(memory_space=pl.ANY)
    return pl.pallas_call(
        kernel,
        out_shape=jax.ShapeDtypeStruct((ROWS, COLS), BF),
        in_specs=[hbm] * 7,
        out_specs=hbm,
        scratch_shapes=[
            pltpu.VMEM((8, XROWS, COLS), BF),
            pltpu.VMEM((16, ROWS, 2 * DEPTH), BF),
            pltpu.VMEM((16, 3, 2 * DEPTH, COLS), BF),
            pltpu.VMEM((2, NZ, 2 * DEPTH, COLS), BF),
            pltpu.VMEM((2, DEPTH, COLS), BF),
            pltpu.VMEM((4, ROWS, COLS), BF),
            pltpu.VMEM((3, ROWS + 8, COLS), F32),
            pltpu.VMEM((ROWS, COLS), F32),
            pltpu.VMEM((ROWS + BLK, COLS), BF),
            pltpu.VMEM((32 * BLK, 2 * BLK), BF),
            pltpu.VMEM((32, 2 * BLK), F32),
            pltpu.VMEM((ROWS, 128), F32),
            pltpu.VMEM((3, 16, COLS), BF),
            pltpu.VMEM((3, 16, COLS), BF),
            pltpu.VMEM((ROWS, COLS), BF),
            pltpu.VMEM((ROWS, COLS), BF),
            pltpu.VMEM((ROWS, COLS), BF),
            pltpu.VMEM((1, COLS), F32),
            pltpu.VMEM((3, 3, COLS), F32),
            pltpu.VMEM((32, BLK), BF),
            pltpu.VMEM((1, COLS), F32),
            dma((7,)),
            dma((14,)), dma((2, 4, 2)),
            dma((24,)), dma((1, 4, 8)),
            dma((50,)), dma((2, 8, 2)), dma((2, 8)),
            dma((60,)), dma((2, 8, 2)), dma((2, 8)),
            dma((1,)), dma((1,)),
            dma((4,)), dma((4,)),
            dma((2,)), dma((2,)),
        ],
        compiler_params=pltpu.CompilerParams(
            collective_id=0, has_side_effects=True, vmem_limit_bytes=58 * 1024 * 1024
        ),
    )(
        tokens,
        norm_gain.reshape(1, COLS),
        jnp.transpose(in_weight, (1, 0, 2)),
        short_weight,
        filters.T,
        skip.reshape(1, COLS),
        out_weight,
    )


def solution(mesh):
    return jax.shard_map(
        body,
        mesh=mesh,
        in_specs=(
            P("ctx", "mp"),
            P("mp"),
            P("ctx", None, "mp"),
            P(None, None, "mp"),
            P(None, "mp"),
            P("mp"),
            P("ctx", "mp"),
        ),
        out_specs=P("ctx", "mp"),
        check_vma=False,
    )
```

```python
import jax
import jax.numpy as jnp
from jax import lax
from jax.experimental import pallas as pl
from jax.experimental.pallas import tpu as pltpu
from jax.sharding import PartitionSpec as P

D = 4096
EPS = 1e-06
NX, NZ, NY = 4, 8, 2
ROWS, COLS, DEPTH = 768, 512, 128
BLK = 128
NB = ROWS // BLK
XROWS = ROWS + 16
HALF = 384
GSIZE = 16
FAR = NZ // 2
PIECES = ((640, 128), (512, 128), (384, 128), (256, 128), (192, 64), (128, 64), (64, 64), (0, 64))
CHUNKS = ((512, 256), (256, 256), (128, 128), (0, 128))
BF = jnp.bfloat16
F32 = jnp.float32


def kernel(
    tok_ref, gain_ref, inw_ref, short_ref, filt_ref, skip_ref, outw_ref,
    out_ref,
    xg, ag, wg, wo, yo, mx, acc, acc2, gated, toep, ext, ss, hs_send, hs_recv,
    part_send, part_recv, out_v, gain_v, short_v, filt_v, skip_v,
    ls, xs, xr, ms, mr, wsend, wrecv, wsib, osend, orecv, osib, ys, yr, ps, pr, hs, hr,
):
    ctx = lax.axis_index("ctx")
    mp = lax.axis_index("mp")
    core = ctx % 2
    z = (ctx // 2) % NZ
    yl = ctx // (2 * NZ)
    x = mp % NX
    yh = mp // NX

    def at(yl_, z_, core_, yh_, x_):
        return ((yl_ * NZ + z_) * 2 + core_, yh_ * NX + x_)

    right = at(yl, z, core, yh, (x + 1) % NX)
    left = at(yl, z, core, yh, (x + NX - 1) % NX)
    across = at(yl, z, core, 1 - yh, x)
    up = at(yl, (z + 1) % NZ, core, yh, x)
    down = at(yl, (z + NZ - 1) % NZ, core, yh, x)
    beside = at(1 - yl, z, core, yh, x)
    corner = at(1 - yl, z, core, 1 - yh, x)
    sib = at(yl, z, 1 - core, yh, x)
    after = ((ctx + 1) % (4 * NZ), mp)
    before = ((ctx + 4 * NZ - 1) % (4 * NZ), mp)

    barrier = pltpu.get_barrier_semaphore()
    everyone = (right, left, across, up, down, beside, corner, sib, after, before)
    for dev in everyone:
        pl.semaphore_signal(barrier, inc=1, device_id=dev, device_id_type=pl.DeviceIdType.MESH)

    own = mp
    row = yl * NZ + z
    my_rows = pl.ds(pl.multiple_of(core * DEPTH, DEPTH), DEPTH)
    loads = [
        pltpu.make_async_copy(src, dst, ls.at[i])
        for i, (src, dst) in enumerate((
            (inw_ref, wg.at[row, :, my_rows, :]),
            (tok_ref, xg.at[own, pl.ds(0, ROWS), :]),
            (gain_ref, gain_v),
            (outw_ref, yo.at[0]),
            (filt_ref, filt_v),
            (short_ref, short_v),
            (skip_ref, skip_v),
        ))
    ]
    for copy in loads:
        copy.start()

    loads[2].wait()
    gain = gain_v[...]
    g_hi = gain.astype(BF).astype(F32)
    g_mid = (gain - g_hi).astype(BF).astype(F32)
    g_lo = gain - g_hi - g_mid
    which = lax.broadcasted_iota(jnp.int32, (16, COLS), 0)
    parts = jnp.where(which == 0, g_hi, jnp.where(which == 1, g_mid, jnp.where(which == 2, g_lo, 0.0)))
    xg[own, ROWS:XROWS, :] = parts.astype(BF)
    loads[0].wait()
    loads[1].wait()

    pl.semaphore_wait(barrier, len(everyone))

    sends = []

    def push(src, dst, ssem, rsem, dev):
        copy = pltpu.make_async_remote_copy(
            src_ref=src, dst_ref=dst, send_sem=ssem, recv_sem=rsem,
            device_id=dev, device_id_type=pl.DeviceIdType.MESH,
        )
        copy.start()
        sends.append(copy)

    def arrived(dst, ssem, rsem):
        pltpu.make_async_remote_copy(
            src_ref=dst, dst_ref=dst, send_sem=ssem, recv_sem=rsem,
            device_id=sib, device_id_type=pl.DeviceIdType.MESH,
        ).wait_recv()

    class Ring:
        def __init__(self, buf, planes, ssem, rsem, pieces):
            self.buf, self.planes = buf, planes
            self.ssem, self.rsem, self.pieces = ssem, rsem, pieces
            self.count = 0

        def slot(self, plane, dx):
            return ((yh + plane) % NY if self.planes == 2 else 0) * NX + (x + dx) % NX

        def view(self, plane, dx, piece):
            begin, size = self.pieces[piece]
            return self.buf.at[self.slot(plane, dx), pl.ds(begin, size), :]

        def send(self, plane, dx, piece, way):
            dev, shift = {"r": (right, 1), "l": (left, NX - 1), "y": (across, 0)}[way]
            there = (1, 0) if way == "y" else (plane, (dx + NX - shift) % NX)
            view = self.view(plane, dx, piece)
            push(
                view, view, self.ssem.at[self.count],
                self.rsem.at[there[0], there[1], piece], dev,
            )
            self.count += 1

        def wait(self, plane, dx, piece):
            arrived(self.view(plane, dx, piece), self.ssem.at[0], self.rsem.at[plane, dx, piece])

    class Column:
        def __init__(self, view_of, ssem, rsem, sibsem):
            self.view_of = view_of
            self.ssem, self.rsem, self.sibsem = ssem, rsem, sibsem
            self.count = 0

        def view(self, plane, dz, parity, part=None):
            begin, size = parity * DEPTH, DEPTH
            if part is not None:
                begin, size = begin + part * (DEPTH // 2), DEPTH // 2
            return self.view_of(plane, (z + dz) % NZ, pl.ds(begin, size))

        def send(self, plane, dz, way, part=None):
            dev, shift = {"u": (up, 1), "d": (down, NZ - 1), "y": (beside, 0), "s": (sib, 0)}[way]
            view = self.view(plane, dz, core, part)
            if way == "s":
                rsem = self.sibsem.at[plane, dz]
            elif way == "y":
                rsem = self.rsem.at[1, dz, part or 0]
            else:
                rsem = self.rsem.at[plane, (dz + NZ - shift) % NZ, part]
            push(view, view, self.ssem.at[self.count], rsem, dev)
            self.count += 1

        def wait(self, plane, dz, part=None):
            arrived(
                self.view(plane, dz, core, part), self.ssem.at[0],
                self.rsem.at[plane, dz, 0 if part is None else part],
            )

        def wait_sib(self, plane, dz):
            arrived(self.view(plane, dz, 1 - core), self.ssem.at[0], self.sibsem.at[plane, dz])

        def start(self, plane):
            for part in (0, 1):
                self.send(plane, 0, "u", part)
                self.send(plane, 0, "d", 1 - part)

        def hop(self, plane, dist):
            end = FAR - 1 if plane == 1 else FAR
            for turn in (0, 1):
                for dz, way, part in ((NZ - dist, "u", turn), (dist, "d", 1 - turn)):
                    self.wait(plane, dz, part)
                    if dist + 1 < end or dist + 1 == end and turn == 0:
                        self.send(plane, dz, way, part)
                    if plane == 0 and dist == FAR - 1 and turn == 1:
                        self.send(plane, dz, "y", part)
            for dz in (NZ - dist, dist):
                self.send(plane, dz, "s")

        def last(self, plane):
            self.wait(plane, FAR, 0)
            self.wait(plane, FAR, 1)
            if plane == 0:
                self.send(0, FAR, "y")
            self.send(plane, FAR, "s")

    tok = Ring(xg, 2, xs, xr, ((0, HALF), (HALF, XROWS - HALF)))
    mix = Ring(mx, 1, ms, mr, PIECES)
    win = Column(
        lambda plane, z_, rows: wg.at[((yl + plane) % NY) * NZ + z_, :, rows, :],
        wsend, wrecv, wsib,
    )
    wout = Column(
        lambda plane, z_, rows: wo.at[(yl + plane) % NY, z_, rows, :],
        osend, orecv, osib,
    )

    tok.send(0, 0, 0, "y")
    win.start(0)
    for half, way in ((0, "r"), (1, "l"), (1, "y"), (1, "r"), (0, "l")):
        tok.send(0, 0, half, way)
    win.send(0, 0, "s")
    for copy in loads[3:]:
        copy.wait()

    acc[...] = jnp.zeros_like(acc)
    ss[...] = jnp.zeros_like(ss)

    def norm(plane, dx):
        slot = tok.slot(plane, dx)
        rows3 = xg[slot, ROWS:XROWS, :].astype(F32)
        g = rows3[0:1] + rows3[1:2] + rows3[2:3]

        @pl.loop(0, NB)
        def _(b):
            rows = pl.ds(pl.multiple_of(b * BLK, BLK), BLK)
            t = xg[slot, rows, :].astype(F32)
            sq = t * t
            ss[rows, :] += (sq[:, 0:128] + sq[:, 128:256]) + (sq[:, 256:384] + sq[:, 384:512])
            a = (t * g).astype(BF)
            ag[2 * slot, rows, :] = a[:, 0:256]
            ag[2 * slot + 1, rows, :] = a[:, 256:512]

    def spread_filters(piece):
        if piece == 0:
            ext[:, 0:BLK] = filt_v[...].astype(F32)
            ext[:, BLK:] = jnp.zeros((ext.shape[0], BLK), F32)

        @pl.loop(8 * piece, 8 * piece + 8)
        def _(g):
            row_ = jnp.broadcast_to(ext[pl.ds(g, 1), :], (2 * BLK, 2 * BLK))
            shifted = pltpu.roll(row_, BLK, 1, stride=1, stride_axis=0)
            toep[pl.ds(pl.multiple_of(g * BLK, BLK), BLK), :] = shifted[:, 0:BLK].T.astype(BF)

    opposite = tok.slot(0, 2)
    opposite_there = tok.slot(1, 2)

    def project(count, q_of, when, begin=0, size=ROWS):
        rows = slice(begin, begin + size)

        @pl.loop(0, count)
        def _(k):
            q = q_of(k)

            @pl.when(when(q))
            def _():
                @pl.loop(0, 3)
                def _(s):
                    acc[s, 8 + begin : 8 + begin + size, :] += jnp.dot(
                        ag[q, rows], wg[q, s], preferred_element_type=F32
                    )

    def project_pair(count, slot_of, when, begin=0, size=ROWS):
        rows = slice(begin, begin + size)

        @pl.loop(0, count)
        def _(k):
            q = 2 * slot_of(k)

            @pl.when(when(slot_of(k)))
            def _():
                a = jnp.concatenate([ag[q, rows], ag[q + 1, rows]], axis=1)

                @pl.loop(0, 3)
                def _(s):
                    w = jnp.concatenate([wg[q, s], wg[q + 1, s]], axis=0)
                    acc[s, 8 + begin : 8 + begin + size, :] += jnp.dot(a, w, preferred_element_type=F32)

    norm(0, 0)
    spread_filters(0)
    win.hop(0, 1)
    win.send(0, 0, "y")
    tok.wait(1, 0, 0)
    tok.send(1, 0, 0, "r")
    tok.send(1, 0, 0, "l")
    spread_filters(1)
    win.hop(0, 2)
    tok.wait(1, 0, 1)
    tok.send(1, 0, 1, "l")
    tok.send(1, 0, 1, "r")
    push(yo.at[0], yo.at[1], ys.at[0], yr.at[0], corner)
    for dx in (NX - 1, 1):
        tok.wait(0, dx, 0)
        tok.wait(0, dx, 1)
        norm(0, dx)
    norm(1, 0)
    spread_filters(2)
    win.hop(0, 3)
    win.wait(1, 0)
    win.start(1)
    win.send(1, 0, "s")
    tok.wait(1, NX - 1, 0)
    tok.send(1, NX - 1, 0, "r")
    tok.send(0, NX - 1, 0, "r")
    spread_filters(3)
    win.last(0)
    for dz in range(NZ):
        win.wait_sib(0, dz)
    beyond = [tok.slot(1, NX - 1), tok.slot(1, 1)]

    def early(slot):
        ok = jnp.logical_and(slot != opposite, slot != opposite_there)
        return jnp.logical_and(ok, jnp.logical_and(slot != beyond[0], slot != beyond[1]))

    project_pair(4, lambda k: yl * (NZ // 2) + k, early)
    tok.wait(1, 1, 0)
    tok.wait(1, 1, 1)
    tok.send(1, 1, 1, "l")
    tok.send(0, 1, 1, "l")
    win.hop(1, 1)
    norm(1, 1)
    tok.wait(1, NX - 1, 1)
    norm(1, NX - 1)
    arrived(yo.at[1], ys.at[0], yr.at[0])
    wo[yl, z, my_rows, :] = jnp.where(yl == yh, yo[0], yo[1])
    wout.send(0, 0, "y")
    project_pair(2, lambda k: (1 - yh) * NX + (x + 1 + 2 * k) % NX, lambda slot: yh != yl)
    for dz in (0, 1, 7):
        win.wait_sib(1, dz)

    def there(k):
        return (1 - yl) * NZ + (z + NZ - 1 + k) % NZ

    project(
        3, there, lambda q: jnp.logical_and(q // 2 != opposite, q // 2 != opposite_there)
    )
    win.hop(1, 2)
    wout.start(0)
    wout.send(0, 0, "s")
    tok.wait(1, 2, 0)
    tok.wait(1, 2, 1)
    norm(1, 2)
    project_pair(1, lambda k: opposite_there, lambda slot: yh != yl)
    project(
        3, there, lambda q: jnp.logical_and(q // 2 == opposite_there, yh == yl)
    )
    win.wait(1, FAR)
    win.send(1, FAR, "s")
    win.wait_sib(1, 2)
    win.wait_sib(1, 6)
    project(
        2, lambda k: (1 - yl) * NZ + (z + 2 + 4 * k) % NZ, lambda q: q // 2 != opposite
    )
    wout.wait(1, 0)
    wout.start(1)
    wout.send(1, 0, "s")
    for dz in (5, 3):
        win.wait(1, dz, 0)
        win.wait(1, dz, 1)
        win.send(1, dz, "s")
    wout.hop(0, 1)
    win.wait_sib(1, FAR)
    project(1, lambda k: (1 - yl) * NZ + (z + FAR) % NZ, lambda q: q // 2 != opposite)
    tok.wait(0, 2, 0)
    tok.wait(0, 2, 1)
    norm(0, 2)
    win.wait_sib(1, 5)
    win.wait_sib(1, 3)

    last_up = (1 - yl) * NZ + (z + FAR + 1) % NZ
    last_down = (1 - yl) * NZ + (z + FAR - 1) % NZ

    def final(begin, size):
        rows = slice(begin, begin + size)
        pieces = [ag[2 * opposite, rows], ag[2 * opposite + 1, rows]]
        for q in (last_up, last_down):
            a = ag[q, rows]
            pieces.append(jnp.where(q // 2 != opposite, a, jnp.zeros_like(a)))
        a = jnp.concatenate(pieces, axis=1)
        scale = lax.rsqrt(jnp.sum(ss[rows, :], axis=1, keepdims=True) / D + EPS)

        @pl.loop(0, 3)
        def _(s):
            w = jnp.concatenate(
                [wg[2 * opposite, s], wg[2 * opposite + 1, s], wg[last_up, s], wg[last_down, s]], axis=0
            )
            there = slice(8 + begin, 8 + begin + size)
            total = acc[s, there, :] + jnp.dot(a, w, preferred_element_type=F32)
            acc[s, there, :] = (total * scale).astype(BF).astype(F32)

    lanes_group = lax.broadcasted_iota(jnp.int32, (BLK, 128), 1) // GSIZE

    def taps(s, b, j):
        cols = slice(128 * j, 128 * (j + 1))
        v = acc[s, pl.ds(pl.multiple_of(b * BLK, BLK), BLK + 8), cols]
        total = short_v[0, s : s + 1, cols] * v
        total = total + short_v[1, s : s + 1, cols] * pltpu.roll(v, 1, 0)
        total = total + short_v[2, s : s + 1, cols] * pltpu.roll(v, 2, 0)
        return total[8:]

    def gate(b):
        for j in range(4):
            kv = taps(1, b, j) * taps(2, b, j)
            gated[pl.ds(pl.multiple_of((b + 1) * BLK, BLK), BLK), 128 * j : 128 * (j + 1)] = kv.astype(BF)

    def combine(b):
        rows = pl.ds(pl.multiple_of(b * BLK, BLK), BLK)
        for j in range(4):
            cols = slice(128 * j, 128 * (j + 1))
            window = gated[pl.ds(pl.multiple_of(b * BLK, BLK), 2 * BLK), cols]
            every = jnp.dot(toep[1024 * j : 1024 * (j + 1), :], window, preferred_element_type=F32)
            medium = every[0:BLK]
            for g in range(1, 8):
                medium = jnp.where(lanes_group == g, every[BLK * g : BLK * (g + 1)], medium)
            direct = window[BLK:].astype(F32)
            mixed = taps(0, b, j) * (medium + skip_v[:, cols] * direct)
            mx[x, rows, cols] = mixed.astype(BF)

    halo_g = (gated.at[pl.ds(ROWS, BLK), :], gated.at[pl.ds(0, BLK), :])

    def halo_out():
        for s in range(3):
            hs_send[s] = acc[s, ROWS - 8 : ROWS + 8, :].astype(BF)
        push(hs_send, hs_recv, hs.at[0], hr.at[0], after)
        push(halo_g[0], halo_g[1], hs.at[1], hr.at[1], after)

    def halo_in():
        arrived(hs_recv, hs.at[0], hr.at[0])
        arrived(halo_g[1], hs.at[1], hr.at[1])
        inside = ctx > 0
        for s in range(3):
            acc[s, 0:8, :] = jnp.where(inside, hs_recv[s].astype(F32)[8:16], 0.0)
        gated[0:BLK, :] = jnp.where(inside, gated[0:BLK, :].astype(F32), 0.0).astype(BF)

    def give(c):
        for piece, way in ((2 * c, "r"), (2 * c + 1, "l"), (2 * c + 1, "r"), (2 * c, "l")):
            mix.send(0, 0, piece, way)

    def relay(c):
        mix.wait(0, NX - 1, 2 * c)
        mix.send(0, NX - 1, 2 * c, "r")
        mix.wait(0, 1, 2 * c + 1)
        mix.send(0, 1, 2 * c + 1, "l")

    final(HALF, HALF)
    gate(5)
    halo_out()
    gate(4)
    combine(5)
    mix.send(0, 0, 0, "r")
    mix.send(0, 0, 0, "l")
    wout.hop(0, 2)
    final(0, HALF)
    gate(3)
    combine(4)
    mix.send(0, 0, 1, "l")
    mix.send(0, 0, 1, "r")
    wout.hop(0, 3)
    wout.hop(1, 1)
    gate(2)
    combine(3)
    gate(1)
    combine(2)
    relay(0)
    give(1)
    wout.last(0)
    halo_in()
    gate(0)
    combine(1)
    combine(0)
    wout.hop(1, 2)
    for dz in (5, 3):
        wout.wait(1, dz, 0)
        wout.wait(1, dz, 1)
        wout.send(1, dz, "s")
    wout.wait(1, FAR)
    wout.send(1, FAR, "s")
    relay(1)
    give(2)
    give(3)

    def product(plane, rows):
        total = None
        for x_ in range(NX):
            w = wo[plane, 2 * x_ : 2 * x_ + 2].reshape(COLS, COLS)
            term = jnp.dot(mx[x_, rows, :], w, preferred_element_type=F32)
            total = term if total is None else total + term
        return total

    def theirs(c):
        for dx, piece in ((NX - 1, 2 * c + 1), (1, 2 * c), (2, 2 * c), (2, 2 * c + 1)):
            mix.wait(0, dx, piece)
        rows = slice(CHUNKS[c][0], sum(CHUNKS[c]))
        there = pl.ds(*CHUNKS[c])
        part_send[rows, :] = product(1 - yh, rows).astype(BF)
        push(part_send.at[there, :], part_recv.at[there, :], ps.at[c], pr.at[c], across)

    def ours(c):
        rows = slice(CHUNKS[c][0], sum(CHUNKS[c]))
        acc2[rows, :] = xg[own, rows, :].astype(F32) + product(yh, rows)

    def finish(c):
        rows = slice(CHUNKS[c][0], sum(CHUNKS[c]))
        there = pl.ds(*CHUNKS[c])
        arrived(part_recv.at[there, :], ps.at[c], pr.at[c])
        out_v[rows, :] = (acc2[rows, :] + part_recv[rows, :].astype(F32)).astype(BF)
        copy = pltpu.make_async_copy(out_v.at[there, :], out_ref.at[there, :], ls.at[c])
        copy.start()
        return copy

    for plane in range(NY):
        for dz in range(NZ):
            wout.wait_sib(plane, dz)
    theirs(0)
    relay(2)
    theirs(1)
    relay(3)
    ours(0)
    ours(1)
    theirs(2)
    theirs(3)
    ours(2)
    ours(3)
    stores = [finish(0), finish(1), finish(2), finish(3)]
    for copy in stores:
        copy.wait()
    for copy in sends:
        copy.wait_send()


def body(tokens, norm_gain, in_weight, short_weight, filters, skip, out_weight):
    dma = pltpu.SemaphoreType.DMA
    hbm = pl.BlockSpec(memory_space=pl.ANY)
    return pl.pallas_call(
        kernel,
        out_shape=jax.ShapeDtypeStruct((ROWS, COLS), BF),
        in_specs=[hbm] * 7,
        out_specs=hbm,
        scratch_shapes=[
            pltpu.VMEM((8, XROWS, COLS), BF),
            pltpu.VMEM((16, ROWS, 2 * DEPTH), BF),
            pltpu.VMEM((16, 3, 2 * DEPTH, COLS), BF),
            pltpu.VMEM((2, NZ, 2 * DEPTH, COLS), BF),
            pltpu.VMEM((2, DEPTH, COLS), BF),
            pltpu.VMEM((4, ROWS, COLS), BF),
            pltpu.VMEM((3, ROWS + 8, COLS), F32),
            pltpu.VMEM((ROWS, COLS), F32),
            pltpu.VMEM((ROWS + BLK, COLS), BF),
            pltpu.VMEM((32 * BLK, 2 * BLK), BF),
            pltpu.VMEM((32, 2 * BLK), F32),
            pltpu.VMEM((ROWS, 128), F32),
            pltpu.VMEM((3, 16, COLS), BF),
            pltpu.VMEM((3, 16, COLS), BF),
            pltpu.VMEM((ROWS, COLS), BF),
            pltpu.VMEM((ROWS, COLS), BF),
            pltpu.VMEM((ROWS, COLS), BF),
            pltpu.VMEM((1, COLS), F32),
            pltpu.VMEM((3, 3, COLS), F32),
            pltpu.VMEM((32, BLK), BF),
            pltpu.VMEM((1, COLS), F32),
            dma((7,)),
            dma((14,)), dma((2, 4, 2)),
            dma((24,)), dma((1, 4, 8)),
            dma((50,)), dma((2, 8, 2)), dma((2, 8)),
            dma((60,)), dma((2, 8, 2)), dma((2, 8)),
            dma((1,)), dma((1,)),
            dma((4,)), dma((4,)),
            dma((2,)), dma((2,)),
        ],
        compiler_params=pltpu.CompilerParams(
            collective_id=0, has_side_effects=True, vmem_limit_bytes=58 * 1024 * 1024
        ),
    )(
        tokens,
        norm_gain.reshape(1, COLS),
        jnp.transpose(in_weight, (1, 0, 2)),
        short_weight,
        filters.T,
        skip.reshape(1, COLS),
        out_weight,
    )


def solution(mesh):
    return jax.shard_map(
        body,
        mesh=mesh,
        in_specs=(
            P("ctx", "mp"),
            P("mp"),
            P("ctx", None, "mp"),
            P(None, None, "mp"),
            P(None, "mp"),
            P("mp"),
            P("ctx", "mp"),
        ),
        out_specs=P("ctx", "mp"),
        check_vma=False,
    )
```
